32 devices in a mesh: fsdp: 4 (over x, core), ctx: 8 (over z, y).
Axes of the slice: x: 2, y: 2, z: 4, core: 2. Of those that a mesh axis runs over, the one named last changes fastest.
Arguments:
- hidden_in: bfloat16 [4, 1024, 576], P('fsdp', 'ctx'), may hold values from -6 to 6
- positions: int32 [4, 1024], P('fsdp', 'ctx'), may hold values from 0 to 1023, as said below
- block_pairs: int32 [4, 8], P('fsdp'), may hold values from 0 to 7, as said below
- norm_gains: bfloat16 [2, 576], P(None, 'ctx'), may hold values from 0.5 to 1.5
- w_query: bfloat16 [576, 576], P('fsdp', 'ctx'), may hold values from -0.25 to 0.25
- w_kv: bfloat16 [576, 384], P('fsdp', 'ctx'), may hold values from -0.25 to 0.25
- w_out: bfloat16 [576, 576], P('fsdp', 'ctx'), may hold values from -4 to 4
- w_gate_up: bfloat16 [576, 3072], P('fsdp', 'ctx'), may hold values from -0.25 to 0.25
- w_down: bfloat16 [1536, 576], P('fsdp', 'ctx'), may hold values from -0.15625 to 0.15625
- output_grad: bfloat16 [4, 1024, 576], P('fsdp', 'ctx'), may hold values from -6 to 6
Outputs:
- hidden_out: bfloat16 [4, 1024, 576], P('fsdp', 'ctx')
- input_grad: float32 [4, 1024, 576], P('fsdp', 'ctx')
- w_query_grad: float32 [576, 576], P('fsdp', 'ctx')
- w_kv_grad: float32 [576, 384], P('fsdp', 'ctx')
- w_out_grad: float32 [576, 576], P('fsdp', 'ctx')
- w_gate_up_grad: float32 [576, 3072], P('fsdp', 'ctx')
- w_down_grad: float32 [1536, 576], P('fsdp', 'ctx')
- gains_grad: float32 [2, 576], P(None, 'ctx')
The draws below stay inside these ranges and needn't reach their ends.
Inputs may be any that keep to these rules, and one draw needn't show every extreme that they name: Each row is a permutation of 0 to 7; context device c holds blocks block_pairs[s, c] and 15 - block_pairs[s, c] of 64 tokens of sequence s, in that order. `positions`: A row's position counts tokens from the start of its document; documents are packed into each sequence in order, sequence 0 is a single document, and rows stand in the dealt order of block_pairs.
All inputs are finite; a program needn't handle non-finite values.
Results may differ from the reference program's by a relative error of at most 0.013.
Values may be sent and summed in bfloat16 or wider, within the bound.
A program may use at most 128 MiB of HBM per device.

```python
import math
import jax
import jax.numpy as jnp
from jax import lax

D = 576
H = 9
KVH = 3
HD = 64
FF = 1536
BLK = 64
QDIM = 576
KVDIM = 192
SEQ_LEN = 1024
SEQS = 4
TOKENS = 4096
N_CTX = 8


def block_times_drawn(pair_row, block_len, ctx_count):
    row_ids = jnp.arange(2 * block_len * ctx_count, dtype=jnp.int32)
    owner_ids = row_ids // (2 * block_len)
    within_ids = row_ids % (2 * block_len)
    first_block = jnp.take(pair_row, owner_ids).astype(jnp.int32)
    block_ids = jnp.where(within_ids < block_len, first_block, 2 * ctx_count - 1 - first_block)
    return (block_ids * block_len + within_ids % block_len).astype(jnp.int32)


def layout_tables(key):
    pair_keys = jax.random.split(jax.random.fold_in(key, 11), SEQS)
    pair_table = jax.vmap(lambda one_key: jax.random.permutation(one_key, N_CTX))(pair_keys).astype(jnp.int32)
    doc_marks = jax.random.randint(jax.random.fold_in(key, 23), (SEQS, SEQ_LEN), 0, max(SEQ_LEN // 4, 2)) == 0
    seq_ids = jnp.broadcast_to(jnp.arange(SEQS, dtype=jnp.int32)[:, None], (SEQS, SEQ_LEN))
    doc_marks = doc_marks & (seq_ids > 0)
    order_ids = jnp.broadcast_to(jnp.arange(SEQ_LEN, dtype=jnp.int32)[None, :], (SEQS, SEQ_LEN))
    starts = jnp.where(doc_marks | (order_ids == 0), order_ids, 0)
    doc_starts = lax.cummax(starts, axis=1)
    seq_positions = order_ids - doc_starts
    dealt_times = jax.vmap(lambda pair_row: block_times_drawn(pair_row, BLK, N_CTX))(pair_table)
    dealt_positions = jnp.take_along_axis(seq_positions, dealt_times, axis=1)
    return (pair_table, dealt_positions.astype(jnp.int32))


def draw_positions(key, part):
    return layout_tables(key)[1]


def draw_block_pairs(key, part):
    return layout_tables(key)[0]


def levels(rng, extent, cuts, smallest, largest):
    def one(axis_at, shards_of):
        draws = jax.random.uniform(jax.random.fold_in(jax.random.fold_in(rng, 6), axis_at), (shards_of,), jnp.float32, smallest / len(cuts), largest / len(cuts))
        return jnp.repeat(jnp.exp(draws), extent[axis_at] // shards_of).reshape((-1,) + (1,) * (len(extent) - axis_at - 1))

    gain = one(*cuts[0])
    for cut in cuts[1:]:
        gain = gain * one(*cut)
    return gain


def normal_values(own_key, shape, scale, limit, shards=(), kind=jnp.bfloat16):
    array = scale * jax.random.normal(own_key, shape, jnp.float32)
    if shards:
        array = array * levels(own_key, shape, shards, -0.22, 0.18)
    return jnp.clip(array, -limit, limit).astype(kind)


def setup_inputs(seed: int = 0) -> dict:
    key_of = jax.random.split(jax.random.key(seed), 11)
    return {
        "hidden_in": normal_values(key_of[0], (SEQS, SEQ_LEN, D), 1.0, 6.0, ((0, 4), (1, 8))),
        "positions": draw_positions(jax.random.fold_in(key_of[10], 71), 0),
        "block_pairs": draw_block_pairs(jax.random.fold_in(key_of[10], 71), 0),
        "norm_gains": jnp.clip(1.0 + 0.1 * jax.random.normal(key_of[3], (2, D), jnp.float32), 0.5, 1.5).astype(jnp.bfloat16),
        "w_query": normal_values(key_of[4], (D, QDIM), D ** -0.5, 0.25, ((0, 4), (1, 8))),
        "w_kv": normal_values(key_of[5], (D, 2 * KVDIM), D ** -0.5, 0.25, ((0, 4), (1, 8))),
        "w_out": normal_values(key_of[6], (QDIM, D), (max(4 * D // SEQ_LEN, 1)) ** -0.5, 4.0, ((0, 4), (1, 8))),
        "w_gate_up": normal_values(key_of[7], (D, 2 * FF), D ** -0.5, 0.25, ((0, 4), (1, 8))),
        "w_down": normal_values(key_of[8], (FF, D), FF ** -0.5, 0.15625, ((0, 4), (1, 8))),
        "output_grad": normal_values(key_of[9], (SEQS, SEQ_LEN, D), 1.0, 6.0, ((0, 4), (1, 8))),
    }


EPSILON = 1e-05
THETA = 100000.0

def block_times(pair_row, block_len, ctx_count):
    row_ids = jnp.arange(2 * block_len * ctx_count, dtype=jnp.int32)
    owner_ids = row_ids // (2 * block_len)
    within_ids = row_ids % (2 * block_len)
    first_block = jnp.take(pair_row, owner_ids).astype(jnp.int32)
    block_ids = jnp.where(within_ids < block_len, first_block, 2 * ctx_count - 1 - first_block)
    return (block_ids * block_len + within_ids % block_len).astype(jnp.int32)

def rope_tables(token_pos, head_size):
    half_size = head_size // 2
    freq_vec = THETA ** (-(jnp.arange(half_size, dtype=jnp.float32) * 2.0) / head_size)
    angles = token_pos.astype(jnp.float32)[:, None] * freq_vec[None, :]
    cos_half = jnp.cos(angles)
    sin_half = jnp.sin(angles)
    return (jnp.concatenate([cos_half, cos_half], 1), jnp.concatenate([sin_half, sin_half], 1))

def rotate(values, cos_table, sin_table, head_count):
    row_count = values.shape[0]
    shaped = values.reshape(row_count, head_count, -1)
    half_size = shaped.shape[2] // 2
    turned = jnp.concatenate([-shaped[:, :, half_size:], shaped[:, :, :half_size]], 2)
    return (shaped * cos_table[:, None, :] + turned * sin_table[:, None, :]).reshape(row_count, -1)

def rotate_back(grad_vals, cos_table, sin_table, head_count):
    row_count = grad_vals.shape[0]
    shaped = grad_vals.reshape(row_count, head_count, -1)
    half_size = shaped.shape[2] // 2
    scaled = shaped * sin_table[:, None, :]
    turned = jnp.concatenate([scaled[:, :, half_size:], -scaled[:, :, :half_size]], 2)
    return (shaped * cos_table[:, None, :] + turned).reshape(row_count, -1)

def norm_forward(values, gain_vec):
    inv_scale = lax.rsqrt(lax.optimization_barrier(jnp.mean(values * values, axis=1, keepdims=True)) + EPSILON)
    return (values * inv_scale * gain_vec[None, :], inv_scale)

def norm_backward(values, inv_scale, gain_vec, grad_out):
    weighted = grad_out * gain_vec[None, :]
    gain_grad = lax.optimization_barrier(jnp.sum(grad_out * values * inv_scale, axis=0))
    inner_mean = lax.optimization_barrier(jnp.mean(weighted * values, axis=1, keepdims=True))
    return (inv_scale * weighted - values * inv_scale ** 3 * inner_mean, gain_grad)

def score_block(query_grp, key_blk, query_time, key_time):
    scores = jnp.einsum('qkgd,skd->kgqs', query_grp.astype(jnp.float32), key_blk.astype(jnp.float32)) * HD ** (-0.5)
    key_mask = key_time[None, None, None, :] <= query_time[None, None, :, None]
    return (scores, key_mask)

def attend(query_b, kv_all, query_time, key_time):
    tok_count = query_b.shape[0]
    length = kv_all.shape[0]
    width = math.gcd(length, 1024)
    block_count = length // width
    group_size = H // KVH
    query_grp = query_b.reshape(tok_count, KVH, group_size, HD)
    kv_blocks = kv_all.reshape(block_count, width, 2, KVH, HD)
    time_blocks = key_time.reshape(block_count, width)

    def total_step(running, block_in):
        kv_blk, time_blk = block_in
        scores, key_mask = score_block(query_grp, kv_blk[:, 0], query_time, time_blk)
        return (running + lax.optimization_barrier(jnp.sum(jnp.where(key_mask, jnp.exp(scores), 0.0), axis=3)), None)
    totals = lax.scan(total_step, jnp.zeros((KVH, group_size, tok_count), jnp.float32), (kv_blocks, time_blocks))[0]
    logsum = jnp.log(totals)

    def output_step(running, block_in):
        kv_blk, time_blk = block_in
        scores, key_mask = score_block(query_grp, kv_blk[:, 0], query_time, time_blk)
        prob_b = jnp.where(key_mask, jnp.exp(scores - logsum[:, :, :, None]), 0.0).astype(jnp.bfloat16)
        part_out = jnp.einsum('kgqs,skd->qkgd', prob_b.astype(jnp.float32), kv_blk[:, 1].astype(jnp.float32))
        return (running + part_out, None)
    attn_out = lax.scan(output_step, jnp.zeros((tok_count, KVH, group_size, HD), jnp.float32), (kv_blocks, time_blocks))[0]
    return (attn_out.reshape(tok_count, -1).astype(jnp.bfloat16), logsum)

def attend_back(query_b, kv_all, query_time, key_time, logsum, attn_b, attn_grad_b):
    tok_count = query_b.shape[0]
    length = kv_all.shape[0]
    width = math.gcd(length, 1024)
    block_count = length // width
    group_size = H // KVH
    query_grp = query_b.reshape(tok_count, KVH, group_size, HD)
    grad_grp = attn_grad_b.reshape(tok_count, KVH, group_size, HD)
    product = attn_grad_b.astype(jnp.float32) * attn_b.astype(jnp.float32)
    delta_sum = lax.optimization_barrier(jnp.sum(product.reshape(tok_count, KVH, group_size, HD), axis=3)).transpose(1, 2, 0)
    kv_blocks = kv_all.reshape(block_count, width, 2, KVH, HD)
    time_blocks = key_time.reshape(block_count, width)

    def back_step(running, block_in):
        kv_blk, time_blk = block_in
        scores, key_mask = score_block(query_grp, kv_blk[:, 0], query_time, time_blk)
        prob_f = jnp.where(key_mask, jnp.exp(scores - logsum[:, :, :, None]), 0.0)
        prob_grad = jnp.einsum('qkgd,skd->kgqs', grad_grp.astype(jnp.float32), kv_blk[:, 1].astype(jnp.float32))
        score_grad = (prob_f * (prob_grad - delta_sum[:, :, :, None]) * HD ** (-0.5)).astype(jnp.bfloat16)
        score_f = score_grad.astype(jnp.float32)
        query_next = running + jnp.einsum('kgqs,skd->qkgd', score_f, kv_blk[:, 0].astype(jnp.float32))
        key_grad = jnp.einsum('kgqs,qkgd->skd', score_f, query_grp.astype(jnp.float32))
        prob_r = prob_f.astype(jnp.bfloat16).astype(jnp.float32)
        value_grad = jnp.einsum('kgqs,qkgd->skd', prob_r, grad_grp.astype(jnp.float32))
        return (query_next, jnp.concatenate([key_grad.reshape(width, -1), value_grad.reshape(width, -1)], 1))
    query_grad, kv_grad = lax.scan(back_step, jnp.zeros((tok_count, KVH, group_size, HD), jnp.float32), (kv_blocks, time_blocks))
    return (query_grad.reshape(tok_count, -1), kv_grad.reshape(length, -1))

def reference(hidden_in, positions, block_pairs, norm_gains, w_query, w_kv, w_out, w_gate_up, w_down, output_grad):
    gain_one = norm_gains[0].astype(jnp.float32)
    gain_two = norm_gains[1].astype(jnp.float32)
    kv_dim = KVH * HD
    q_width = math.gcd(SEQ_LEN, 1024)
    q_count = SEQ_LEN // q_width
    wq_grad = jnp.zeros((D, QDIM), jnp.float32)
    wkv_grad = jnp.zeros((D, 2 * kv_dim), jnp.float32)
    wo_grad = jnp.zeros((QDIM, D), jnp.float32)
    wgu_grad = jnp.zeros((D, 2 * FF), jnp.float32)
    wdown_grad = jnp.zeros((FF, D), jnp.float32)
    gone_grad = jnp.zeros((D,), jnp.float32)
    gtwo_grad = jnp.zeros((D,), jnp.float32)
    results = []
    input_grads = []
    for seq_id in range(SEQS):
        rows_in = hidden_in[seq_id].astype(jnp.float32)
        normed_one, scale_one = norm_forward(rows_in, gain_one)
        normed_one_b = normed_one.astype(jnp.bfloat16)
        query = jnp.dot(normed_one_b, w_query, preferred_element_type=jnp.float32)
        kv_proj = jnp.dot(normed_one_b, w_kv, preferred_element_type=jnp.float32)
        cos_table, sin_table = rope_tables(positions[seq_id], HD)
        query_b = rotate(query, cos_table, sin_table, H).astype(jnp.bfloat16)
        key_b = rotate(kv_proj[:, :kv_dim], cos_table, sin_table, KVH).astype(jnp.bfloat16)
        kv_all = jnp.concatenate([key_b, kv_proj[:, kv_dim:].astype(jnp.bfloat16)], 1)
        key_time = block_times(block_pairs[seq_id], BLK, N_CTX)
        query_blocks = query_b.reshape(q_count, q_width, -1)
        time_query = key_time.reshape(q_count, q_width)
        attn_blocks, logsum_blocks = lax.map(lambda block_item: attend(block_item[0], kv_all, block_item[1], key_time), (query_blocks, time_query))
        attn_b = attn_blocks.reshape(SEQ_LEN, -1)
        mixed = rows_in + jnp.dot(attn_b, w_out, preferred_element_type=jnp.float32)
        normed_two, scale_two = norm_forward(mixed, gain_two)
        normed_two_b = normed_two.astype(jnp.bfloat16)
        gate_up = jnp.dot(normed_two_b, w_gate_up, preferred_element_type=jnp.float32)
        gate_part = gate_up[:, :FF]
        up_part = gate_up[:, FF:]
        sig_gate = jax.nn.sigmoid(gate_part)
        silu_gate = gate_part * sig_gate
        act_b = (silu_gate * up_part).astype(jnp.bfloat16)
        results.append((mixed + jnp.dot(act_b, w_down, preferred_element_type=jnp.float32)).astype(jnp.bfloat16))
        grad_b = output_grad[seq_id]
        act_grad = jnp.dot(grad_b, w_down.T, preferred_element_type=jnp.float32)
        wdown_grad = wdown_grad + jnp.dot(act_b.T, grad_b, preferred_element_type=jnp.float32)
        gate_grad = act_grad * up_part * sig_gate * (1.0 + gate_part * (1.0 - sig_gate))
        gu_grad_b = jnp.concatenate([gate_grad, act_grad * silu_gate], 1).astype(jnp.bfloat16)
        wgu_grad = wgu_grad + jnp.dot(normed_two_b.T, gu_grad_b, preferred_element_type=jnp.float32)
        normed_two_grad = jnp.dot(gu_grad_b, w_gate_up.T, preferred_element_type=jnp.float32)
        mixed_back, gain_term_two = norm_backward(mixed, scale_two, gain_two, normed_two_grad)
        gtwo_grad = gtwo_grad + gain_term_two
        mixed_grad = grad_b.astype(jnp.float32) + mixed_back
        mixed_grad_b = mixed_grad.astype(jnp.bfloat16)
        wo_grad = wo_grad + jnp.dot(attn_b.T, mixed_grad_b, preferred_element_type=jnp.float32)
        attn_grad_b = jnp.dot(mixed_grad_b, w_out.T, preferred_element_type=jnp.float32).astype(jnp.bfloat16)

        def back_block(kv_total, block_item):
            query_blk, time_blk, lse_blk, attn_blk, grad_blk = block_item
            query_part, kv_part = attend_back(query_blk, kv_all, time_blk, key_time, lse_blk, attn_blk, grad_blk)
            return (kv_total + kv_part, query_part)
        kv_grad, query_parts = lax.scan(back_block, jnp.zeros((SEQ_LEN, 2 * kv_dim), jnp.float32), (query_blocks, time_query, logsum_blocks, attn_blocks, attn_grad_b.reshape(q_count, q_width, -1)))
        query_grad = query_parts.reshape(SEQ_LEN, -1)
        query_pre = rotate_back(query_grad, cos_table, sin_table, H).astype(jnp.bfloat16)
        key_pre = rotate_back(kv_grad[:, :kv_dim], cos_table, sin_table, KVH)
        kv_pre = jnp.concatenate([key_pre, kv_grad[:, kv_dim:]], 1).astype(jnp.bfloat16)
        wq_grad = wq_grad + jnp.dot(normed_one_b.T, query_pre, preferred_element_type=jnp.float32)
        wkv_grad = wkv_grad + jnp.dot(normed_one_b.T, kv_pre, preferred_element_type=jnp.float32)
        normed_one_grad = jnp.dot(query_pre, w_query.T, preferred_element_type=jnp.float32) + jnp.dot(kv_pre, w_kv.T, preferred_element_type=jnp.float32)
        rows_back, gain_term_one = norm_backward(rows_in, scale_one, gain_one, normed_one_grad)
        gone_grad = gone_grad + gain_term_one
        input_grads.append(mixed_grad + rows_back)
    grad_scale = TOKENS ** (-0.5)
    gains_grad = jnp.stack([gone_grad, gtwo_grad]) * grad_scale
    return (jnp.stack(results), jnp.stack(input_grads), wq_grad * grad_scale, wkv_grad * grad_scale, wo_grad * grad_scale, wgu_grad * grad_scale, wdown_grad * grad_scale, gains_grad)
```

```python
import functools
import math

import jax
import jax.numpy as jnp
from jax import lax
from jax.experimental import pallas as pl
from jax.experimental.pallas import tpu as pltpu
from jax.sharding import PartitionSpec as P

H = 9
KVH = 3
HD = 64
FF = 1536


EPSILON = 1e-05
THETA = 100000.0

MESH_ID = pl.DeviceIdType.MESH
PAIR = 2


def greet(peers):
    barrier = pltpu.get_barrier_semaphore()
    for peer in peers:
        pl.semaphore_signal(barrier, inc=1, device_id=peer, device_id_type=MESH_ID)
    pl.semaphore_wait(barrier, len(peers))


class Place:
    def __init__(self, fsdp, ctx):
        self.nk, self.nx = PAIR, fsdp // PAIR
        self.ny, self.nz = PAIR, ctx // PAIR
        f = lax.axis_index("fsdp")
        c = lax.axis_index("ctx")
        self.f, self.c = f, c
        self.x, self.k = f // self.nk, f % self.nk
        self.z, self.y = c // self.ny, c % self.ny

    def rel(self, dx=0, dk=0, dz=0, dy=0):
        fx = (self.x + dx) % self.nx if dx else self.x
        fk = (self.k + dk) % self.nk if dk else self.k
        cz = (self.z + dz) % self.nz if dz else self.z
        cy = (self.y + dy) % self.ny if dy else self.y
        return (fx * self.nk + fk, cz * self.ny + cy)

    def peers(self):
        return (
            [self.rel(dx=d) for d in range(1, self.nx)]
            + [self.rel(dk=d) for d in range(1, self.nk)]
            + [self.rel(dz=d) for d in range(1, self.nz)]
            + [self.rel(dy=d) for d in range(1, self.ny)]
        )


def gather_kernel(fsdp, ctx, w_ref, h_ref, wout, hout, wsend, wrecv, hsend, hrecv, own_sem):
    me = Place(fsdp, ctx)
    nx, nk, nz, ny = me.nx, me.nk, me.nz, me.ny
    own_w = pltpu.make_async_copy(w_ref, wout.at[me.f, me.c], own_sem.at[0])
    own_h = pltpu.make_async_copy(h_ref, hout.at[me.c], own_sem.at[1])
    own_w.start()
    own_h.start()
    greet(me.peers())
    sends = []

    def push_w(kx, kk, kz, ky, stage, step, src=None):
        f, c = me.rel(dx=kx, dk=kk, dz=kz, dy=ky)
        offs = {stage: step}
        dest = me.rel(**offs)
        new = dict(dx=kx, dk=kk, dz=kz, dy=ky)
        size = dict(dx=nx, dk=nk, dz=nz, dy=ny)[stage]
        new[stage] = (new[stage] - step) % size
        slot = ((new["dx"] * nk + new["dk"]) * nz + new["dz"]) * ny + new["dy"]
        copy = pltpu.make_async_remote_copy(
            src_ref=wout.at[f, c] if src is None else src,
            dst_ref=wout.at[f, c],
            send_sem=wsend.at[slot],
            recv_sem=wrecv.at[slot],
            device_id=dest,
            device_id_type=MESH_ID,
        )
        copy.start()
        sends.append(copy)

    def wait_w(kx, kk, kz, ky):
        f, c = me.rel(dx=kx, dk=kk, dz=kz, dy=ky)
        slot = ((kx * nk + kk) * nz + kz) * ny + ky
        pltpu.make_async_remote_copy(
            src_ref=wout.at[f, c],
            dst_ref=wout.at[f, c],
            send_sem=wsend.at[slot],
            recv_sem=wrecv.at[slot],
            device_id=me.rel(dk=1),
            device_id_type=MESH_ID,
        ).wait_recv()

    def push_h(kz, ky, stage, step, src=None):
        c = me.rel(dz=kz, dy=ky)[1]
        dest = me.rel(**{stage: step})
        new = dict(dz=kz, dy=ky)
        new[stage] = (new[stage] - step) % dict(dz=nz, dy=ny)[stage]
        slot = new["dz"] * ny + new["dy"]
        copy = pltpu.make_async_remote_copy(
            src_ref=hout.at[c] if src is None else src,
            dst_ref=hout.at[c],
            send_sem=hsend.at[slot],
            recv_sem=hrecv.at[slot],
            device_id=dest,
            device_id_type=MESH_ID,
        )
        copy.start()
        sends.append(copy)

    def wait_h(kz, ky):
        c = me.rel(dz=kz, dy=ky)[1]
        slot = kz * ny + ky
        pltpu.make_async_remote_copy(
            src_ref=hout.at[c],
            dst_ref=hout.at[c],
            send_sem=hsend.at[slot],
            recv_sem=hrecv.at[slot],
            device_id=me.rel(dk=1),
            device_id_type=MESH_ID,
        ).wait_recv()

    for d in range(1, nx):
        push_w(0, 0, 0, 0, "dx", d, w_ref)
    for d in range(1, nz):
        push_w(0, 0, 0, 0, "dz", d, w_ref)
    for d in range(1, ny):
        push_w(0, 0, 0, 0, "dy", d, w_ref)
    for d in range(1, nk):
        push_w(0, 0, 0, 0, "dk", d, w_ref)
    for d in range(1, nz):
        push_h(0, 0, "dz", d, h_ref)
    for d in range(1, ny):
        push_h(0, 0, "dy", d, h_ref)
    for kz in range(1, nz):
        wait_w(0, 0, kz, 0)
        for d in range(1, nx):
            push_w(0, 0, kz, 0, "dx", d)
        for d in range(1, ny):
            push_w(0, 0, kz, 0, "dy", d)
        for d in range(1, nk):
            push_w(0, 0, kz, 0, "dk", d)
    for ky in range(1, ny):
        for kz in range(nz):
            wait_w(0, 0, kz, ky)
            for d in range(1, nx):
                push_w(0, 0, kz, ky, "dx", d)
            for d in range(1, nk):
                push_w(0, 0, kz, ky, "dk", d)
    for kz in range(1, nz):
        wait_h(kz, 0)
        for d in range(1, ny):
            push_h(kz, 0, "dy", d)
    for ky in range(1, ny):
        for kz in range(nz):
            wait_h(kz, ky)
    for kx in range(1, nx):
        for ky in range(ny):
            for kz in range(nz):
                wait_w(kx, 0, kz, ky)
                for d in range(1, nk):
                    push_w(kx, 0, kz, ky, "dk", d)
    for kk in range(1, nk):
        for kx in range(nx):
            for ky in range(ny):
                for kz in range(nz):
                    wait_w(kx, kk, kz, ky)
    for copy in sends:
        copy.wait_send()
    own_w.wait()
    own_h.wait()


def gather_all(packed, rows):
    fsdp, ctx = lax.axis_size("fsdp"), lax.axis_size("ctx")
    return pl.pallas_call(
        functools.partial(gather_kernel, fsdp, ctx),
        out_shape=(
            jax.ShapeDtypeStruct((fsdp, ctx) + packed.shape, packed.dtype),
            jax.ShapeDtypeStruct((ctx,) + rows.shape, rows.dtype),
        ),
        in_specs=[pl.BlockSpec(memory_space=pltpu.VMEM)] * 2,
        out_specs=[pl.BlockSpec(memory_space=pl.ANY)] * 2,
        scratch_shapes=[
            pltpu.SemaphoreType.DMA((fsdp * ctx,)),
            pltpu.SemaphoreType.DMA((fsdp * ctx,)),
            pltpu.SemaphoreType.DMA((ctx,)),
            pltpu.SemaphoreType.DMA((ctx,)),
            pltpu.SemaphoreType.DMA((2,)),
        ],
        compiler_params=pltpu.CompilerParams(collective_id=0, has_side_effects=True),
    )(packed, rows)


def exchange_kernel(ctx, part_ref, out_ref, held, send_sem, recv_sem):
    f, c = lax.axis_index("fsdp"), lax.axis_index("ctx")
    greet([(f, (c + d) % ctx) for d in range(1, ctx)])
    copies = []
    for d in range(1, ctx):
        to = (c + d) % ctx
        copy = pltpu.make_async_remote_copy(
            src_ref=part_ref.at[to],
            dst_ref=held.at[d - 1],
            send_sem=send_sem.at[d - 1],
            recv_sem=recv_sem.at[d - 1],
            device_id=(f, to),
            device_id_type=MESH_ID,
        )
        copy.start()
        copies.append(copy)
    total = part_ref[c].astype(jnp.float32)
    for d in range(1, ctx):
        copies[d - 1].wait_recv()
        total = total + held[d - 1].astype(jnp.float32)
    out_ref[...] = total
    for copy in copies:
        copy.wait_send()


def exchange_sum(parts):
    ctx = lax.axis_size("ctx")
    return pl.pallas_call(
        functools.partial(exchange_kernel, ctx),
        out_shape=jax.ShapeDtypeStruct(parts.shape[1:], jnp.float32),
        in_specs=[pl.BlockSpec(memory_space=pltpu.VMEM)],
        out_specs=pl.BlockSpec(memory_space=pltpu.VMEM),
        scratch_shapes=[
            pltpu.VMEM((ctx - 1,) + parts.shape[1:], parts.dtype),
            pltpu.SemaphoreType.DMA((ctx - 1,)),
            pltpu.SemaphoreType.DMA((ctx - 1,)),
        ],
        compiler_params=pltpu.CompilerParams(
            collective_id=1, has_side_effects=True, vmem_limit_bytes=48 * 2**20
        ),
    )(parts)


def scatter_kernel(
    fsdp, ctx, g_ref, out_ref, held_k, held_x, held_y, held_z, send, recv_k, recv_x, recv_y, recv_z
):
    me = Place(fsdp, ctx)
    nx, nz, ny = me.nx, me.nz, me.ny
    greet(me.peers())
    sends = []

    def push(src, dst, dst_sem, dest):
        copy = pltpu.make_async_remote_copy(
            src_ref=src,
            dst_ref=dst,
            send_sem=send.at[len(sends)],
            recv_sem=dst_sem,
            device_id=dest,
            device_id_type=MESH_ID,
        )
        copy.start()
        sends.append(copy)

    def wait(ref, sem):
        pltpu.make_async_remote_copy(
            src_ref=ref,
            dst_ref=ref,
            send_sem=sem,
            recv_sem=sem,
            device_id=me.rel(dk=1),
            device_id_type=MESH_ID,
        ).wait_recv()

    order_x = list(range(1, nx)) + [0]
    order_c = [(dy, dz) for dy in list(range(1, ny)) + [0] for dz in list(range(1, nz)) + [0]]
    for dx in order_x:
        for dy, dz in order_c:
            f, c = me.rel(dx=dx, dk=1, dz=dz, dy=dy)
            slot = (dx * nz + dz) * ny + dy
            push(g_ref.at[f, c], held_k.at[slot], recv_k.at[slot], me.rel(dk=1))

    def local_sum(dx, dz, dy):
        f, c = me.rel(dx=dx, dz=dz, dy=dy)
        slot = (dx * nz + dz) * ny + dy
        wait(held_k.at[slot], recv_k.at[slot])
        return g_ref[f, c].astype(jnp.float32) + held_k[slot].astype(jnp.float32), slot

    for dx in order_x[:-1]:
        for dy, dz in order_c:
            total, slot = local_sum(dx, dz, dy)
            held_k[slot] = total.astype(held_k.dtype)
            there = ((dx - 1) * nz + dz) * ny + dy
            push(held_k.at[slot], held_x.at[there], recv_x.at[there], me.rel(dx=dx))

    def x_sum(dz, dy):
        total, slot = local_sum(0, dz, dy)
        for dx in range(1, nx):
            there = ((dx - 1) * nz + dz) * ny + dy
            wait(held_x.at[there], recv_x.at[there])
            total = total + held_x[there].astype(jnp.float32)
        return total, slot

    for dy in range(1, ny):
        for dz in list(range(1, nz)) + [0]:
            total, slot = x_sum(dz, dy)
            held_k[slot] = total.astype(held_k.dtype)
            there = (dy - 1) * nz + dz
            push(held_k.at[slot], held_y.at[there], recv_y.at[there], me.rel(dy=dy))

    def y_sum(dz):
        total, slot = x_sum(dz, 0)
        for dy in range(1, ny):
            there = (dy - 1) * nz + dz
            wait(held_y.at[there], recv_y.at[there])
            total = total + held_y[there].astype(jnp.float32)
        return total, slot

    for dz in range(1, nz):
        total, slot = y_sum(dz)
        held_k[slot] = total.astype(held_k.dtype)
        push(held_k.at[slot], held_z.at[dz - 1], recv_z.at[dz - 1], me.rel(dz=dz))
    total, slot = y_sum(0)
    for dz in range(1, nz):
        wait(held_z.at[dz - 1], recv_z.at[dz - 1])
        total = total + held_z[dz - 1].astype(jnp.float32)
    out_ref[...] = total
    for copy in sends:
        copy.wait_send()


def scatter_sum(grads):
    fsdp, ctx, rows, lanes = grads.shape
    nx, nz, ny = fsdp // PAIR, ctx // PAIR, PAIR
    counts = (nx * ctx, (nx - 1) * ctx, (ny - 1) * nz, nz - 1)
    return pl.pallas_call(
        functools.partial(scatter_kernel, fsdp, ctx),
        out_shape=jax.ShapeDtypeStruct((rows, lanes), jnp.float32),
        in_specs=[pl.BlockSpec(memory_space=pltpu.VMEM)],
        out_specs=pl.BlockSpec(memory_space=pltpu.VMEM),
        scratch_shapes=[pltpu.VMEM((n, rows, lanes), grads.dtype) for n in counts]
        + [pltpu.SemaphoreType.DMA((n,)) for n in (sum(counts),) + counts],
        compiler_params=pltpu.CompilerParams(
            collective_id=2, has_side_effects=True, vmem_limit_bytes=48 * 2**20
        ),
    )(grads)


def unfold(pieces, row_count, col_count):
    fsdp, ctx = pieces.shape[:2]
    shaped = pieces.reshape(fsdp, ctx, row_count, col_count)
    return shaped.transpose(0, 2, 1, 3).reshape(fsdp * row_count, ctx * col_count)


def fold(whole, fsdp, ctx):
    row_count, col_count = whole.shape
    shaped = whole.reshape(fsdp, row_count // fsdp, ctx, col_count // ctx)
    return shaped.transpose(0, 2, 1, 3)


def block_times(pair_row, block_len, ctx_count):
    row_ids = jnp.arange(2 * block_len * ctx_count, dtype=jnp.int32)
    owner_ids = row_ids // (2 * block_len)
    within_ids = row_ids % (2 * block_len)
    first_block = jnp.take(pair_row, owner_ids)
    block_ids = jnp.where(within_ids < block_len, first_block, 2 * ctx_count - 1 - first_block)
    return block_ids * block_len + within_ids % block_len


def rope_tables(token_pos, head_size):
    half_size = head_size // 2
    freq_vec = THETA ** (-(jnp.arange(half_size, dtype=jnp.float32) * 2.0) / head_size)
    angles = token_pos.astype(jnp.float32)[:, None] * freq_vec[None, :]
    cos_half = jnp.cos(angles)
    sin_half = jnp.sin(angles)
    return (jnp.concatenate([cos_half, cos_half], 1), jnp.concatenate([sin_half, sin_half], 1))


def rotate(values, cos_table, sin_table, head_count):
    row_count = values.shape[0]
    shaped = values.reshape(row_count, head_count, -1)
    half_size = shaped.shape[2] // 2
    turned = jnp.concatenate([-shaped[:, :, half_size:], shaped[:, :, :half_size]], 2)
    return (shaped * cos_table[:, None, :] + turned * sin_table[:, None, :]).reshape(row_count, -1)


def rotate_back(grad_vals, cos_table, sin_table, head_count):
    row_count = grad_vals.shape[0]
    shaped = grad_vals.reshape(row_count, head_count, -1)
    half_size = shaped.shape[2] // 2
    scaled = shaped * sin_table[:, None, :]
    turned = jnp.concatenate([scaled[:, :, half_size:], -scaled[:, :, :half_size]], 2)
    return (shaped * cos_table[:, None, :] + turned).reshape(row_count, -1)


def norm_forward(values, gain_vec):
    inv_scale = lax.rsqrt(jnp.mean(values * values, axis=1, keepdims=True) + EPSILON)
    return (values * inv_scale * gain_vec[None, :], inv_scale)


def norm_backward(values, inv_scale, gain_vec, grad_out):
    weighted = grad_out * gain_vec[None, :]
    gain_grad = jnp.sum(grad_out * values * inv_scale, axis=0)
    inner_mean = jnp.mean(weighted * values, axis=1, keepdims=True)
    return (inv_scale * weighted - values * inv_scale**3 * inner_mean, gain_grad)


def score_block(query_grp, key_blk, query_time, key_time):
    scores = jnp.einsum(
        "qkgd,skd->kgqs", query_grp, key_blk, preferred_element_type=jnp.float32
    ) * HD ** (-0.5)
    key_mask = key_time[None, None, None, :] <= query_time[None, None, :, None]
    return (scores, key_mask)


def attend(query_b, kv_all, query_time, key_time):
    tok_count = query_b.shape[0]
    length = kv_all.shape[0]
    width = math.gcd(length, 1024)
    block_count = length // width
    group_size = H // KVH
    query_grp = query_b.reshape(tok_count, KVH, group_size, HD)
    kv_blocks = kv_all.reshape(block_count, width, 2, KVH, HD)
    time_blocks = key_time.reshape(block_count, width)

    def total_step(running, block_in):
        kv_blk, time_blk = block_in
        scores, key_mask = score_block(query_grp, kv_blk[:, 0], query_time, time_blk)
        return (running + jnp.sum(jnp.where(key_mask, jnp.exp(scores), 0.0), axis=3), None)

    totals = lax.scan(
        total_step, jnp.zeros((KVH, group_size, tok_count), jnp.float32), (kv_blocks, time_blocks)
    )[0]
    logsum = jnp.log(totals)

    def output_step(running, block_in):
        kv_blk, time_blk = block_in
        scores, key_mask = score_block(query_grp, kv_blk[:, 0], query_time, time_blk)
        prob_b = jnp.where(key_mask, jnp.exp(scores - logsum[:, :, :, None]), 0.0).astype(
            jnp.bfloat16
        )
        part_out = jnp.einsum(
            "kgqs,skd->qkgd", prob_b, kv_blk[:, 1], preferred_element_type=jnp.float32
        )
        return (running + part_out, None)

    attn_out = lax.scan(
        output_step,
        jnp.zeros((tok_count, KVH, group_size, HD), jnp.float32),
        (kv_blocks, time_blocks),
    )[0]
    return (attn_out.reshape(tok_count, -1).astype(jnp.bfloat16), logsum)


def attend_back(query_b, kv_all, query_time, key_time, logsum, attn_b, attn_grad_b):
    tok_count = query_b.shape[0]
    length = kv_all.shape[0]
    width = math.gcd(length, 1024)
    block_count = length // width
    group_size = H // KVH
    query_grp = query_b.reshape(tok_count, KVH, group_size, HD)
    grad_grp = attn_grad_b.reshape(tok_count, KVH, group_size, HD)
    product = attn_grad_b.astype(jnp.float32) * attn_b.astype(jnp.float32)
    delta_sum = jnp.sum(product.reshape(tok_count, KVH, group_size, HD), axis=3).transpose(1, 2, 0)
    kv_blocks = kv_all.reshape(block_count, width, 2, KVH, HD)
    time_blocks = key_time.reshape(block_count, width)

    def back_step(running, block_in):
        kv_blk, time_blk = block_in
        scores, key_mask = score_block(query_grp, kv_blk[:, 0], query_time, time_blk)
        prob_f = jnp.where(key_mask, jnp.exp(scores - logsum[:, :, :, None]), 0.0)
        prob_grad = jnp.einsum(
            "qkgd,skd->kgqs", grad_grp, kv_blk[:, 1], preferred_element_type=jnp.float32
        )
        score_grad = (prob_f * (prob_grad - delta_sum[:, :, :, None]) * HD ** (-0.5)).astype(
            jnp.bfloat16
        )
        query_next = running + jnp.einsum(
            "kgqs,skd->qkgd", score_grad, kv_blk[:, 0], preferred_element_type=jnp.float32
        )
        key_grad = jnp.einsum(
            "kgqs,qkgd->skd", score_grad, query_grp, preferred_element_type=jnp.float32
        )
        value_grad = jnp.einsum(
            "kgqs,qkgd->skd",
            prob_f.astype(jnp.bfloat16),
            grad_grp,
            preferred_element_type=jnp.float32,
        )
        return (
            query_next,
            jnp.concatenate([key_grad.reshape(width, -1), value_grad.reshape(width, -1)], 1),
        )

    query_grad, kv_grad = lax.scan(
        back_step,
        jnp.zeros((tok_count, KVH, group_size, HD), jnp.float32),
        (kv_blocks, time_blocks),
    )
    return (query_grad.reshape(tok_count, -1), kv_grad.reshape(length, -1))


def body(
    hidden_in,
    positions,
    block_pairs,
    norm_gains,
    w_query,
    w_kv,
    w_out,
    w_gate_up,
    w_down,
    output_grad,
):
    tok_count = hidden_in.shape[1]
    ctx_count = lax.axis_size("ctx")
    block_len = tok_count // 2
    kv_dim = KVH * HD
    grad_scale = 1.0 / math.sqrt(lax.axis_size("fsdp") * ctx_count * tok_count)
    fsdp_count = lax.axis_size("fsdp")
    width = hidden_in.shape[2]
    row_d, col_q = w_query.shape
    col_k, col_o, col_g = w_kv.shape[1], w_out.shape[1], w_gate_up.shape[1]
    lanes, col_d = w_down.shape
    small = jnp.concatenate([w_query, w_kv, w_out], 1)
    gain_flat = norm_gains.reshape(-1)
    n_gu = row_d * col_g // lanes
    n_small = small.size // lanes
    n_gain = -(-gain_flat.size // lanes)
    cut_down, cut_small = n_gu + col_d, n_gu + col_d + n_small
    n_rows = -(-(cut_small + n_gain) // 16) * 16
    gain_rows = jnp.pad(gain_flat, (0, (n_rows - cut_small) * lanes - gain_flat.size))
    packed = jnp.concatenate(
        [
            w_gate_up.reshape(n_gu, lanes),
            w_down.T,
            small.reshape(n_small, lanes),
            gain_rows.reshape(-1, lanes),
        ],
        0,
    )
    pos_cols = jnp.stack([positions[0] // 128, positions[0] % 128], 1).astype(jnp.bfloat16)
    spare = (-(width + 2)) % 128
    rows_b = jnp.concatenate([hidden_in[0], jnp.pad(pos_cols, ((0, 0), (0, spare)))], 1)
    gathered, rows_all = gather_all(packed, rows_b)
    wgu_full = unfold(gathered[:, :, :n_gu], row_d, col_g)
    wdown_t = gathered[:, :, n_gu:cut_down].transpose(1, 2, 0, 3).reshape(ctx_count * col_d, -1)
    small_all = gathered[:, :, cut_down:cut_small].reshape(fsdp_count, ctx_count, row_d, -1)
    wq_full = unfold(small_all[:, :, :, :col_q], row_d, col_q)
    wkv_full = unfold(small_all[:, :, :, col_q : col_q + col_k], row_d, col_k)
    wo_full = unfold(small_all[:, :, :, col_q + col_k :], row_d, col_o)
    gain_all = gathered[0, :, cut_small:].reshape(ctx_count, -1)[:, : gain_flat.size]
    gain_all = gain_all.reshape(ctx_count, 2, -1).transpose(1, 0, 2).reshape(2, -1)
    gain_one = gain_all[0].astype(jnp.float32)
    gain_two = gain_all[1].astype(jnp.float32)
    rows_in = hidden_in[0].astype(jnp.float32)
    normed_one, scale_one = norm_forward(rows_in, gain_one)
    normed_one_b = normed_one.astype(jnp.bfloat16)
    query = jnp.dot(normed_one_b, wq_full, preferred_element_type=jnp.float32)
    cos_table, sin_table = rope_tables(positions[0], HD)
    query_b = rotate(query, cos_table, sin_table, H).astype(jnp.bfloat16)
    rows_all = rows_all.reshape(ctx_count * tok_count, -1)
    normed_all = norm_forward(rows_all[:, :width].astype(jnp.float32), gain_one)[0]
    kv_proj = jnp.dot(
        normed_all.astype(jnp.bfloat16), wkv_full, preferred_element_type=jnp.float32
    )
    pos_all = rows_all[:, width : width + 2].astype(jnp.float32)
    cos_all, sin_all = rope_tables(pos_all[:, 0] * 128.0 + pos_all[:, 1], HD)
    key_b = rotate(kv_proj[:, :kv_dim], cos_all, sin_all, KVH).astype(jnp.bfloat16)
    kv_all = jnp.concatenate([key_b, kv_proj[:, kv_dim:].astype(jnp.bfloat16)], 1)
    key_time = block_times(block_pairs[0], block_len, ctx_count)
    query_time = lax.dynamic_slice_in_dim(key_time, lax.axis_index("ctx") * tok_count, tok_count)
    attn_b, logsum = attend(query_b, kv_all, query_time, key_time)
    mixed = rows_in + jnp.dot(attn_b, wo_full, preferred_element_type=jnp.float32)
    normed_two, scale_two = norm_forward(mixed, gain_two)
    normed_two_b = normed_two.astype(jnp.bfloat16)
    gate_up = jnp.dot(normed_two_b, wgu_full, preferred_element_type=jnp.float32)
    gate_part = gate_up[:, :FF]
    up_part = gate_up[:, FF:]
    sig_gate = jax.nn.sigmoid(gate_part)
    silu_gate = gate_part * sig_gate
    act_b = (silu_gate * up_part).astype(jnp.bfloat16)
    down_out = jnp.einsum("tf,df->td", act_b, wdown_t, preferred_element_type=jnp.float32)
    result = (mixed + down_out).astype(jnp.bfloat16)
    grad_b = output_grad[0]
    act_grad = jnp.einsum("td,df->tf", grad_b, wdown_t, preferred_element_type=jnp.float32)
    wdown_grad_t = jnp.einsum("td,tf->df", grad_b, act_b, preferred_element_type=jnp.float32)
    gate_grad = act_grad * up_part * sig_gate * (1.0 + gate_part * (1.0 - sig_gate))
    gu_grad_b = jnp.concatenate([gate_grad, act_grad * silu_gate], 1).astype(jnp.bfloat16)
    wgu_grad = jnp.einsum("td,tf->df", normed_two_b, gu_grad_b, preferred_element_type=jnp.float32)
    normed_two_grad = jnp.einsum(
        "tf,df->td", gu_grad_b, wgu_full, preferred_element_type=jnp.float32
    )
    mixed_back, gain_term_two = norm_backward(mixed, scale_two, gain_two, normed_two_grad)
    mixed_grad = grad_b.astype(jnp.float32) + mixed_back
    mixed_grad_b = mixed_grad.astype(jnp.bfloat16)
    wo_grad = jnp.einsum("tq,td->qd", attn_b, mixed_grad_b, preferred_element_type=jnp.float32)
    attn_grad_b = jnp.einsum(
        "td,qd->tq", mixed_grad_b, wo_full, preferred_element_type=jnp.float32
    ).astype(jnp.bfloat16)
    query_grad, kv_terms = attend_back(
        query_b, kv_all, query_time, key_time, logsum, attn_b, attn_grad_b
    )
    kv_grad = exchange_sum(
        kv_terms.reshape(ctx_count, tok_count, 2 * kv_dim).astype(jnp.bfloat16)
    )
    query_pre = rotate_back(query_grad, cos_table, sin_table, H).astype(jnp.bfloat16)
    key_pre = rotate_back(kv_grad[:, :kv_dim], cos_table, sin_table, KVH)
    kv_pre = jnp.concatenate([key_pre, kv_grad[:, kv_dim:]], 1).astype(jnp.bfloat16)
    wq_grad = jnp.einsum("td,tq->dq", normed_one_b, query_pre, preferred_element_type=jnp.float32)
    wkv_grad = jnp.einsum("td,tk->dk", normed_one_b, kv_pre, preferred_element_type=jnp.float32)
    normed_one_grad = jnp.einsum(
        "tq,dq->td", query_pre, wq_full, preferred_element_type=jnp.float32
    ) + jnp.einsum("tk,dk->td", kv_pre, wkv_full, preferred_element_type=jnp.float32)
    rows_back, gain_term_one = norm_backward(rows_in, scale_one, gain_one, normed_one_grad)
    input_grad = mixed_grad + rows_back
    small_grads = jnp.concatenate(
        [fold(g.astype(jnp.bfloat16), fsdp_count, ctx_count) for g in (wq_grad, wkv_grad, wo_grad)],
        3,
    )
    gain_grads = jnp.stack([gain_term_one, gain_term_two]).reshape(2, ctx_count, -1)
    gain_grads = gain_grads.transpose(1, 0, 2).reshape(ctx_count, -1).astype(jnp.bfloat16)
    gain_pad = (n_rows - cut_small) * lanes - gain_flat.size
    gain_grads = jnp.pad(gain_grads, ((0, 0), (0, gain_pad))).reshape(1, ctx_count, -1, lanes)
    down_pieces = wdown_grad_t.astype(jnp.bfloat16).reshape(ctx_count, col_d, fsdp_count, lanes)
    pieces = jnp.concatenate(
        [
            fold(wgu_grad.astype(jnp.bfloat16), fsdp_count, ctx_count).reshape(
                fsdp_count, ctx_count, n_gu, lanes
            ),
            down_pieces.transpose(2, 0, 1, 3),
            small_grads.reshape(fsdp_count, ctx_count, n_small, lanes),
            jnp.broadcast_to(gain_grads, (fsdp_count,) + gain_grads.shape[1:]),
        ],
        2,
    )
    owned = scatter_sum(pieces) * grad_scale
    small_owned = owned[cut_down:cut_small].reshape(row_d, -1)
    owned_grads = (
        small_owned[:, :col_q],
        small_owned[:, col_q : col_q + col_k],
        small_owned[:, col_q + col_k :],
        owned[:n_gu].reshape(row_d, col_g),
        owned[n_gu:cut_down].T,
    )
    gains_owned = owned[cut_small:].reshape(-1)[: gain_flat.size].reshape(2, -1)
    return (
        result[None],
        input_grad[None],
        owned_grads[0],
        owned_grads[1],
        owned_grads[2],
        owned_grads[3],
        owned_grads[4],
        gains_owned,
    )


def solution(mesh):
    return jax.shard_map(
        body,
        mesh=mesh,
        in_specs=(
            P("fsdp", "ctx", None),
            P("fsdp", "ctx"),
            P("fsdp", None),
            P(None, "ctx"),
            P("fsdp", "ctx"),
            P("fsdp", "ctx"),
            P("fsdp", "ctx"),
            P("fsdp", "ctx"),
            P("fsdp", "ctx"),
            P("fsdp", "ctx", None),
        ),
        out_specs=(
            P("fsdp", "ctx", None),
            P("fsdp", "ctx", None),
            P("fsdp", "ctx"),
            P("fsdp", "ctx"),
            P("fsdp", "ctx"),
            P("fsdp", "ctx"),
            P("fsdp", "ctx"),
            P(None, "ctx"),
        ),
        check_vma=False,
    )
```

```python
import functools
import math

import jax
import jax.numpy as jnp
from jax import lax
from jax.experimental import pallas as pl
from jax.experimental.pallas import tpu as pltpu
from jax.sharding import PartitionSpec as P

H = 9
KVH = 3
HD = 64
FF = 1536


EPSILON = 1e-05
THETA = 100000.0

MESH_ID = pl.DeviceIdType.MESH
PAIR = 2


def greet(peers):
    barrier = pltpu.get_barrier_semaphore()
    for peer in peers:
        pl.semaphore_signal(barrier, inc=1, device_id=peer, device_id_type=MESH_ID)
    pl.semaphore_wait(barrier, len(peers))


class Place:
    def __init__(self, fsdp, ctx):
        self.nk, self.nx = PAIR, fsdp // PAIR
        self.ny, self.nz = PAIR, ctx // PAIR
        f = lax.axis_index("fsdp")
        c = lax.axis_index("ctx")
        self.f, self.c = f, c
        self.x, self.k = f // self.nk, f % self.nk
        self.z, self.y = c // self.ny, c % self.ny

    def rel(self, dx=0, dk=0, dz=0, dy=0):
        fx = (self.x + dx) % self.nx if dx else self.x
        fk = (self.k + dk) % self.nk if dk else self.k
        cz = (self.z + dz) % self.nz if dz else self.z
        cy = (self.y + dy) % self.ny if dy else self.y
        return (fx * self.nk + fk, cz * self.ny + cy)

    def peers(self):
        return (
            [self.rel(dx=d) for d in range(1, self.nx)]
            + [self.rel(dk=d) for d in range(1, self.nk)]
            + [self.rel(dz=d) for d in range(1, self.nz)]
            + [self.rel(dy=d) for d in range(1, self.ny)]
        )


def gather_kernel(fsdp, ctx, w_ref, h_ref, wout, hout, wsend, wrecv, hsend, hrecv, own_sem):
    me = Place(fsdp, ctx)
    nx, nk, nz, ny = me.nx, me.nk, me.nz, me.ny
    own_w = pltpu.make_async_copy(w_ref, wout.at[me.f, me.c], own_sem.at[0])
    own_h = pltpu.make_async_copy(h_ref, hout.at[me.c], own_sem.at[1])
    own_w.start()
    own_h.start()
    greet(me.peers())
    sends = []

    def push_w(kx, kk, kz, ky, stage, step, src=None):
        f, c = me.rel(dx=kx, dk=kk, dz=kz, dy=ky)
        offs = {stage: step}
        dest = me.rel(**offs)
        new = dict(dx=kx, dk=kk, dz=kz, dy=ky)
        size = dict(dx=nx, dk=nk, dz=nz, dy=ny)[stage]
        new[stage] = (new[stage] - step) % size
        slot = ((new["dx"] * nk + new["dk"]) * nz + new["dz"]) * ny + new["dy"]
        copy = pltpu.make_async_remote_copy(
            src_ref=wout.at[f, c] if src is None else src,
            dst_ref=wout.at[f, c],
            send_sem=wsend.at[slot],
            recv_sem=wrecv.at[slot],
            device_id=dest,
            device_id_type=MESH_ID,
        )
        copy.start()
        sends.append(copy)

    def wait_w(kx, kk, kz, ky):
        f, c = me.rel(dx=kx, dk=kk, dz=kz, dy=ky)
        slot = ((kx * nk + kk) * nz + kz) * ny + ky
        pltpu.make_async_remote_copy(
            src_ref=wout.at[f, c],
            dst_ref=wout.at[f, c],
            send_sem=wsend.at[slot],
            recv_sem=wrecv.at[slot],
            device_id=me.rel(dk=1),
            device_id_type=MESH_ID,
        ).wait_recv()

    def push_h(kz, ky, stage, step, src=None):
        c = me.rel(dz=kz, dy=ky)[1]
        dest = me.rel(**{stage: step})
        new = dict(dz=kz, dy=ky)
        new[stage] = (new[stage] - step) % dict(dz=nz, dy=ny)[stage]
        slot = new["dz"] * ny + new["dy"]
        copy = pltpu.make_async_remote_copy(
            src_ref=hout.at[c] if src is None else src,
            dst_ref=hout.at[c],
            send_sem=hsend.at[slot],
            recv_sem=hrecv.at[slot],
            device_id=dest,
            device_id_type=MESH_ID,
        )
        copy.start()
        sends.append(copy)

    def wait_h(kz, ky):
        c = me.rel(dz=kz, dy=ky)[1]
        slot = kz * ny + ky
        pltpu.make_async_remote_copy(
            src_ref=hout.at[c],
            dst_ref=hout.at[c],
            send_sem=hsend.at[slot],
            recv_sem=hrecv.at[slot],
            device_id=me.rel(dk=1),
            device_id_type=MESH_ID,
        ).wait_recv()

    for d in range(1, nx):
        push_w(0, 0, 0, 0, "dx", d, w_ref)
    for d in range(1, nz):
        push_w(0, 0, 0, 0, "dz", d, w_ref)
    for d in range(1, ny):
        push_w(0, 0, 0, 0, "dy", d, w_ref)
    for d in range(1, nk):
        push_w(0, 0, 0, 0, "dk", d, w_ref)
    for d in range(1, nz):
        push_h(0, 0, "dz", d, h_ref)
    for d in range(1, ny):
        push_h(0, 0, "dy", d, h_ref)
    for kz in range(1, nz):
        wait_w(0, 0, kz, 0)
        for d in range(1, nx):
            push_w(0, 0, kz, 0, "dx", d)
        for d in range(1, ny):
            push_w(0, 0, kz, 0, "dy", d)
        for d in range(1, nk):
            push_w(0, 0, kz, 0, "dk", d)
    for ky in range(1, ny):
        for kz in range(nz):
            wait_w(0, 0, kz, ky)
            for d in range(1, nx):
                push_w(0, 0, kz, ky, "dx", d)
            for d in range(1, nk):
                push_w(0, 0, kz, ky, "dk", d)
    for kz in range(1, nz):
        wait_h(kz, 0)
        for d in range(1, ny):
            push_h(kz, 0, "dy", d)
    for ky in range(1, ny):
        for kz in range(nz):
            wait_h(kz, ky)
    for kx in range(1, nx):
        for ky in range(ny):
            for kz in range(nz):
                wait_w(kx, 0, kz, ky)
                for d in range(1, nk):
                    push_w(kx, 0, kz, ky, "dk", d)
    for kk in range(1, nk):
        for kx in range(nx):
            for ky in range(ny):
                for kz in range(nz):
                    wait_w(kx, kk, kz, ky)
    for copy in sends:
        copy.wait_send()
    own_w.wait()
    own_h.wait()


def gather_all(packed, rows):
    fsdp, ctx = lax.axis_size("fsdp"), lax.axis_size("ctx")
    return pl.pallas_call(
        functools.partial(gather_kernel, fsdp, ctx),
        out_shape=(
            jax.ShapeDtypeStruct((fsdp, ctx) + packed.shape, packed.dtype),
            jax.ShapeDtypeStruct((ctx,) + rows.shape, rows.dtype),
        ),
        in_specs=[pl.BlockSpec(memory_space=pltpu.VMEM)] * 2,
        out_specs=[pl.BlockSpec(memory_space=pl.ANY)] * 2,
        scratch_shapes=[
            pltpu.SemaphoreType.DMA((fsdp * ctx,)),
            pltpu.SemaphoreType.DMA((fsdp * ctx,)),
            pltpu.SemaphoreType.DMA((ctx,)),
            pltpu.SemaphoreType.DMA((ctx,)),
            pltpu.SemaphoreType.DMA((2,)),
        ],
        compiler_params=pltpu.CompilerParams(collective_id=0, has_side_effects=True),
    )(packed, rows)


def exchange_kernel(fsdp, ctx, part_ref, out_ref, held_y, held_z, send, recv_y, recv_z):
    me = Place(fsdp, ctx)
    nz, ny = me.nz, me.ny
    greet(
        [me.rel(dz=d) for d in range(1, nz)] + [me.rel(dy=d) for d in range(1, ny)],
    )
    sends = []
    y_copies, z_copies = {}, {}
    order_z = list(range(1, nz)) + [0]
    for dz in order_z:
        for dy in range(1, ny):
            slot = (dy - 1) * nz + dz
            copy = pltpu.make_async_remote_copy(
                src_ref=part_ref.at[me.rel(dz=dz, dy=dy)[1]],
                dst_ref=held_y.at[slot],
                send_sem=send.at[len(sends)],
                recv_sem=recv_y.at[slot],
                device_id=me.rel(dy=dy),
                device_id_type=MESH_ID,
            )
            copy.start()
            sends.append(copy)
            y_copies[dz, dy] = copy

    def y_sum(dz):
        total = part_ref[me.rel(dz=dz)[1]].astype(jnp.float32)
        for dy in range(1, ny):
            y_copies[dz, dy].wait_recv()
            total = total + held_y[(dy - 1) * nz + dz].astype(jnp.float32)
        return total

    for dz in range(1, nz):
        held_y[dz] = y_sum(dz).astype(held_y.dtype)
        copy = pltpu.make_async_remote_copy(
            src_ref=held_y.at[dz],
            dst_ref=held_z.at[dz - 1],
            send_sem=send.at[len(sends)],
            recv_sem=recv_z.at[dz - 1],
            device_id=me.rel(dz=dz),
            device_id_type=MESH_ID,
        )
        copy.start()
        sends.append(copy)
        z_copies[dz] = copy
    total = y_sum(0)
    for dz in range(1, nz):
        z_copies[dz].wait_recv()
        total = total + held_z[dz - 1].astype(jnp.float32)
    out_ref[...] = total
    for copy in sends:
        copy.wait_send()


def exchange_sum(parts):
    fsdp, ctx = lax.axis_size("fsdp"), lax.axis_size("ctx")
    counts = ((PAIR - 1) * (ctx // PAIR), ctx // PAIR - 1)
    return pl.pallas_call(
        functools.partial(exchange_kernel, fsdp, ctx),
        out_shape=jax.ShapeDtypeStruct(parts.shape[1:], jnp.float32),
        in_specs=[pl.BlockSpec(memory_space=pltpu.VMEM)],
        out_specs=pl.BlockSpec(memory_space=pltpu.VMEM),
        scratch_shapes=[pltpu.VMEM((n,) + parts.shape[1:], parts.dtype) for n in counts]
        + [pltpu.SemaphoreType.DMA((n,)) for n in (sum(counts),) + counts],
        compiler_params=pltpu.CompilerParams(
            collective_id=1, has_side_effects=True, vmem_limit_bytes=48 * 2**20
        ),
    )(parts)


def scatter_kernel(
    fsdp, ctx, g_ref, out_ref, held_k, held_x, held_y, held_z, send, recv_k, recv_x, recv_y, recv_z
):
    me = Place(fsdp, ctx)
    nx, nz, ny = me.nx, me.nz, me.ny
    greet(me.peers())
    sends = []

    def push(src, dst, dst_sem, dest):
        copy = pltpu.make_async_remote_copy(
            src_ref=src,
            dst_ref=dst,
            send_sem=send.at[len(sends)],
            recv_sem=dst_sem,
            device_id=dest,
            device_id_type=MESH_ID,
        )
        copy.start()
        sends.append(copy)

    def wait(ref, sem):
        pltpu.make_async_remote_copy(
            src_ref=ref,
            dst_ref=ref,
            send_sem=sem,
            recv_sem=sem,
            device_id=me.rel(dk=1),
            device_id_type=MESH_ID,
        ).wait_recv()

    order_x = list(range(1, nx)) + [0]
    order_c = [(dy, dz) for dy in list(range(1, ny)) + [0] for dz in list(range(1, nz)) + [0]]
    for dx in order_x:
        for dy, dz in order_c:
            f, c = me.rel(dx=dx, dk=1, dz=dz, dy=dy)
            slot = (dx * nz + dz) * ny + dy
            push(g_ref.at[f, c], held_k.at[slot], recv_k.at[slot], me.rel(dk=1))

    def local_sum(dx, dz, dy):
        f, c = me.rel(dx=dx, dz=dz, dy=dy)
        slot = (dx * nz + dz) * ny + dy
        wait(held_k.at[slot], recv_k.at[slot])
        return g_ref[f, c].astype(jnp.float32) + held_k[slot].astype(jnp.float32), slot

    for dx in order_x[:-1]:
        for dy, dz in order_c:
            total, slot = local_sum(dx, dz, dy)
            held_k[slot] = total.astype(held_k.dtype)
            there = ((dx - 1) * nz + dz) * ny + dy
            push(held_k.at[slot], held_x.at[there], recv_x.at[there], me.rel(dx=dx))

    def x_sum(dz, dy):
        total, slot = local_sum(0, dz, dy)
        for dx in range(1, nx):
            there = ((dx - 1) * nz + dz) * ny + dy
            wait(held_x.at[there], recv_x.at[there])
            total = total + held_x[there].astype(jnp.float32)
        return total, slot

    for dy in range(1, ny):
        for dz in list(range(1, nz)) + [0]:
            total, slot = x_sum(dz, dy)
            held_k[slot] = total.astype(held_k.dtype)
            there = (dy - 1) * nz + dz
            push(held_k.at[slot], held_y.at[there], recv_y.at[there], me.rel(dy=dy))

    def y_sum(dz):
        total, slot = x_sum(dz, 0)
        for dy in range(1, ny):
            there = (dy - 1) * nz + dz
            wait(held_y.at[there], recv_y.at[there])
            total = total + held_y[there].astype(jnp.float32)
        return total, slot

    for dz in range(1, nz):
        total, slot = y_sum(dz)
        held_k[slot] = total.astype(held_k.dtype)
        push(held_k.at[slot], held_z.at[dz - 1], recv_z.at[dz - 1], me.rel(dz=dz))
    total, slot = y_sum(0)
    for dz in range(1, nz):
        wait(held_z.at[dz - 1], recv_z.at[dz - 1])
        total = total + held_z[dz - 1].astype(jnp.float32)
    out_ref[...] = total
    for copy in sends:
        copy.wait_send()


def scatter_sum(grads):
    fsdp, ctx, rows, lanes = grads.shape
    nx, nz, ny = fsdp // PAIR, ctx // PAIR, PAIR
    counts = (nx * ctx, (nx - 1) * ctx, (ny - 1) * nz, nz - 1)
    return pl.pallas_call(
        functools.partial(scatter_kernel, fsdp, ctx),
        out_shape=jax.ShapeDtypeStruct((rows, lanes), jnp.float32),
        in_specs=[pl.BlockSpec(memory_space=pltpu.VMEM)],
        out_specs=pl.BlockSpec(memory_space=pltpu.VMEM),
        scratch_shapes=[pltpu.VMEM((n, rows, lanes), grads.dtype) for n in counts]
        + [pltpu.SemaphoreType.DMA((n,)) for n in (sum(counts),) + counts],
        compiler_params=pltpu.CompilerParams(
            collective_id=2, has_side_effects=True, vmem_limit_bytes=48 * 2**20
        ),
    )(grads)


def unfold(pieces, row_count, col_count):
    fsdp, ctx = pieces.shape[:2]
    shaped = pieces.reshape(fsdp, ctx, row_count, col_count)
    return shaped.transpose(0, 2, 1, 3).reshape(fsdp * row_count, ctx * col_count)


def fold(whole, fsdp, ctx):
    row_count, col_count = whole.shape
    shaped = whole.reshape(fsdp, row_count // fsdp, ctx, col_count // ctx)
    return shaped.transpose(0, 2, 1, 3)


def block_times(pair_row, block_len, ctx_count):
    within_ids = jnp.arange(2 * block_len, dtype=jnp.int32)[None, :]
    first_block = pair_row[:, None]
    block_ids = jnp.where(within_ids < block_len, first_block, 2 * ctx_count - 1 - first_block)
    return (block_ids * block_len + within_ids % block_len).reshape(-1)


def rope_tables(token_pos, head_size):
    half_size = head_size // 2
    freq_vec = THETA ** (-(jnp.arange(half_size, dtype=jnp.float32) * 2.0) / head_size)
    angles = token_pos.astype(jnp.float32)[:, None] * freq_vec[None, :]
    cos_half = jnp.cos(angles)
    sin_half = jnp.sin(angles)
    return (jnp.concatenate([cos_half, cos_half], 1), jnp.concatenate([sin_half, sin_half], 1))


def rotate(values, cos_table, sin_table, head_count):
    row_count = values.shape[0]
    shaped = values.reshape(row_count, head_count, -1)
    half_size = shaped.shape[2] // 2
    turned = jnp.concatenate([-shaped[:, :, half_size:], shaped[:, :, :half_size]], 2)
    return (shaped * cos_table[:, None, :] + turned * sin_table[:, None, :]).reshape(row_count, -1)


def rotate_back(grad_vals, cos_table, sin_table, head_count):
    row_count = grad_vals.shape[0]
    shaped = grad_vals.reshape(row_count, head_count, -1)
    half_size = shaped.shape[2] // 2
    scaled = shaped * sin_table[:, None, :]
    turned = jnp.concatenate([scaled[:, :, half_size:], -scaled[:, :, :half_size]], 2)
    return (shaped * cos_table[:, None, :] + turned).reshape(row_count, -1)


def norm_forward(values, gain_vec):
    inv_scale = lax.rsqrt(jnp.mean(values * values, axis=1, keepdims=True) + EPSILON)
    return (values * inv_scale * gain_vec[None, :], inv_scale)


def norm_backward(values, inv_scale, gain_vec, grad_out):
    weighted = grad_out * gain_vec[None, :]
    gain_grad = jnp.sum(grad_out * values * inv_scale, axis=0)
    inner_mean = jnp.mean(weighted * values, axis=1, keepdims=True)
    return (inv_scale * weighted - values * inv_scale**3 * inner_mean, gain_grad)


def score_block(query_grp, key_blk, query_time, key_time):
    scores = jnp.einsum(
        "qkgd,skd->kgqs", query_grp, key_blk, preferred_element_type=jnp.float32
    ) * HD ** (-0.5)
    key_mask = key_time[None, None, None, :] <= query_time[None, None, :, None]
    return (scores, key_mask)


def attend(query_b, kv_all, query_time, key_time):
    tok_count = query_b.shape[0]
    length = kv_all.shape[0]
    width = math.gcd(length, 1024)
    block_count = length // width
    group_size = H // KVH
    query_grp = query_b.reshape(tok_count, KVH, group_size, HD)
    kv_blocks = kv_all.reshape(block_count, width, 2, KVH, HD)
    time_blocks = key_time.reshape(block_count, width)

    def total_step(running, block_in):
        kv_blk, time_blk = block_in
        scores, key_mask = score_block(query_grp, kv_blk[:, 0], query_time, time_blk)
        return (running + jnp.sum(jnp.where(key_mask, jnp.exp(scores), 0.0), axis=3), None)

    totals = lax.scan(
        total_step, jnp.zeros((KVH, group_size, tok_count), jnp.float32), (kv_blocks, time_blocks)
    )[0]
    logsum = jnp.log(totals)

    def output_step(running, block_in):
        kv_blk, time_blk = block_in
        scores, key_mask = score_block(query_grp, kv_blk[:, 0], query_time, time_blk)
        prob_b = jnp.where(key_mask, jnp.exp(scores - logsum[:, :, :, None]), 0.0).astype(
            jnp.bfloat16
        )
        part_out = jnp.einsum(
            "kgqs,skd->qkgd", prob_b, kv_blk[:, 1], preferred_element_type=jnp.float32
        )
        return (running + part_out, None)

    attn_out = lax.scan(
        output_step,
        jnp.zeros((tok_count, KVH, group_size, HD), jnp.float32),
        (kv_blocks, time_blocks),
    )[0]
    return (attn_out.reshape(tok_count, -1).astype(jnp.bfloat16), logsum)


def attend_back(query_b, kv_all, query_time, key_time, logsum, attn_b, attn_grad_b):
    tok_count = query_b.shape[0]
    length = kv_all.shape[0]
    width = math.gcd(length, 1024)
    block_count = length // width
    group_size = H // KVH
    query_grp = query_b.reshape(tok_count, KVH, group_size, HD)
    grad_grp = attn_grad_b.reshape(tok_count, KVH, group_size, HD)
    product = attn_grad_b.astype(jnp.float32) * attn_b.astype(jnp.float32)
    delta_sum = jnp.sum(product.reshape(tok_count, KVH, group_size, HD), axis=3).transpose(1, 2, 0)
    kv_blocks = kv_all.reshape(block_count, width, 2, KVH, HD)
    time_blocks = key_time.reshape(block_count, width)

    def back_step(running, block_in):
        kv_blk, time_blk = block_in
        scores, key_mask = score_block(query_grp, kv_blk[:, 0], query_time, time_blk)
        prob_f = jnp.where(key_mask, jnp.exp(scores - logsum[:, :, :, None]), 0.0)
        prob_grad = jnp.einsum(
            "qkgd,skd->kgqs", grad_grp, kv_blk[:, 1], preferred_element_type=jnp.float32
        )
        score_grad = (prob_f * (prob_grad - delta_sum[:, :, :, None]) * HD ** (-0.5)).astype(
            jnp.bfloat16
        )
        query_next = running + jnp.einsum(
            "kgqs,skd->qkgd", score_grad, kv_blk[:, 0], preferred_element_type=jnp.float32
        )
        key_grad = jnp.einsum(
            "kgqs,qkgd->skd", score_grad, query_grp, preferred_element_type=jnp.float32
        )
        value_grad = jnp.einsum(
            "kgqs,qkgd->skd",
            prob_f.astype(jnp.bfloat16),
            grad_grp,
            preferred_element_type=jnp.float32,
        )
        return (
            query_next,
            jnp.concatenate([key_grad.reshape(width, -1), value_grad.reshape(width, -1)], 1),
        )

    query_grad, kv_grad = lax.scan(
        back_step,
        jnp.zeros((tok_count, KVH, group_size, HD), jnp.float32),
        (kv_blocks, time_blocks),
    )
    return (query_grad.reshape(tok_count, -1), kv_grad.reshape(length, -1))


def body(
    hidden_in,
    positions,
    block_pairs,
    norm_gains,
    w_query,
    w_kv,
    w_out,
    w_gate_up,
    w_down,
    output_grad,
):
    tok_count = hidden_in.shape[1]
    ctx_count = lax.axis_size("ctx")
    block_len = tok_count // 2
    kv_dim = KVH * HD
    grad_scale = 1.0 / math.sqrt(lax.axis_size("fsdp") * ctx_count * tok_count)
    fsdp_count = lax.axis_size("fsdp")
    width = hidden_in.shape[2]
    row_d, col_q = w_query.shape
    col_k, col_o, col_g = w_kv.shape[1], w_out.shape[1], w_gate_up.shape[1]
    lanes, col_d = w_down.shape
    small = jnp.concatenate([w_query.T, w_kv.T, w_out.T], 0)
    gain_flat = norm_gains.reshape(-1)
    n_gu = row_d * col_g // lanes
    n_small = small.size // lanes
    n_gain = -(-gain_flat.size // lanes)
    cut_down, cut_small = n_gu + col_d, n_gu + col_d + n_small
    n_rows = -(-(cut_small + n_gain) // 16) * 16
    gain_rows = jnp.pad(gain_flat, (0, (n_rows - cut_small) * lanes - gain_flat.size))
    packed = jnp.concatenate(
        [
            w_gate_up.reshape(n_gu, lanes),
            w_down.T,
            small.reshape(n_small, lanes),
            gain_rows.reshape(-1, lanes),
        ],
        0,
    )
    pos_cols = jnp.stack([positions[0] // 128, positions[0] % 128], 1).astype(jnp.bfloat16)
    spare = (-(width + 2)) % 128
    rows_b = jnp.concatenate([hidden_in[0], jnp.pad(pos_cols, ((0, 0), (0, spare)))], 1)
    gathered, rows_all = gather_all(packed, rows_b)
    wgu_full = unfold(gathered[:, :, :n_gu], row_d, col_g)
    wdown_t = gathered[:, :, n_gu:cut_down].transpose(1, 2, 0, 3).reshape(ctx_count * col_d, -1)
    col_s = small.shape[0]
    small_all = gathered[:, :, cut_down:cut_small].reshape(fsdp_count, ctx_count, col_s, row_d)
    small_all = small_all.transpose(1, 2, 0, 3).reshape(ctx_count, col_s, fsdp_count * row_d)
    wq_t = small_all[:, :col_q].reshape(ctx_count * col_q, -1)
    wkv_t = small_all[:, col_q : col_q + col_k].reshape(ctx_count * col_k, -1)
    wo_t = small_all[:, col_q + col_k :].reshape(ctx_count * col_o, -1)
    gain_all = gathered[0, :, cut_small:].reshape(ctx_count, -1)[:, : gain_flat.size]
    gain_all = gain_all.reshape(ctx_count, 2, -1).transpose(1, 0, 2).reshape(2, -1)
    gain_one = gain_all[0].astype(jnp.float32)
    gain_two = gain_all[1].astype(jnp.float32)
    rows_in = hidden_in[0].astype(jnp.float32)
    normed_one, scale_one = norm_forward(rows_in, gain_one)
    normed_one_b = normed_one.astype(jnp.bfloat16)
    query = jnp.einsum("td,qd->tq", normed_one_b, wq_t, preferred_element_type=jnp.float32)
    cos_table, sin_table = rope_tables(positions[0], HD)
    query_b = rotate(query, cos_table, sin_table, H).astype(jnp.bfloat16)
    rows_all = rows_all.reshape(ctx_count * tok_count, -1)
    normed_all = norm_forward(rows_all[:, :width].astype(jnp.float32), gain_one)[0]
    kv_proj = jnp.einsum(
        "td,kd->tk", normed_all.astype(jnp.bfloat16), wkv_t, preferred_element_type=jnp.float32
    )
    pos_all = rows_all[:, width : width + 2].astype(jnp.float32)
    cos_all, sin_all = rope_tables(pos_all[:, 0] * 128.0 + pos_all[:, 1], HD)
    key_b = rotate(kv_proj[:, :kv_dim], cos_all, sin_all, KVH).astype(jnp.bfloat16)
    kv_all = jnp.concatenate([key_b, kv_proj[:, kv_dim:].astype(jnp.bfloat16)], 1)
    key_time = block_times(block_pairs[0], block_len, ctx_count)
    query_time = lax.dynamic_slice_in_dim(key_time, lax.axis_index("ctx") * tok_count, tok_count)
    attn_b, logsum = attend(query_b, kv_all, query_time, key_time)
    mixed = rows_in + jnp.einsum("tq,dq->td", attn_b, wo_t, preferred_element_type=jnp.float32)
    normed_two, scale_two = norm_forward(mixed, gain_two)
    normed_two_b = normed_two.astype(jnp.bfloat16)
    gate_up = jnp.dot(normed_two_b, wgu_full, preferred_element_type=jnp.float32)
    gate_part = gate_up[:, :FF]
    up_part = gate_up[:, FF:]
    sig_gate = jax.nn.sigmoid(gate_part)
    silu_gate = gate_part * sig_gate
    act_b = (silu_gate * up_part).astype(jnp.bfloat16)
    down_out = jnp.einsum("tf,df->td", act_b, wdown_t, preferred_element_type=jnp.float32)
    result = (mixed + down_out).astype(jnp.bfloat16)
    grad_b = output_grad[0]
    act_grad = jnp.einsum("td,df->tf", grad_b, wdown_t, preferred_element_type=jnp.float32)
    wdown_grad_t = jnp.einsum("td,tf->df", grad_b, act_b, preferred_element_type=jnp.float32)
    gate_grad = act_grad * up_part * sig_gate * (1.0 + gate_part * (1.0 - sig_gate))
    gu_grad_b = jnp.concatenate([gate_grad, act_grad * silu_gate], 1).astype(jnp.bfloat16)
    wgu_grad = jnp.einsum("td,tf->df", normed_two_b, gu_grad_b, preferred_element_type=jnp.float32)
    normed_two_grad = jnp.einsum(
        "tf,df->td", gu_grad_b, wgu_full, preferred_element_type=jnp.float32
    )
    mixed_back, gain_term_two = norm_backward(mixed, scale_two, gain_two, normed_two_grad)
    mixed_grad = grad_b.astype(jnp.float32) + mixed_back
    mixed_grad_b = mixed_grad.astype(jnp.bfloat16)
    wo_grad_t = jnp.einsum("td,tq->dq", mixed_grad_b, attn_b, preferred_element_type=jnp.float32)
    attn_grad_b = jnp.einsum(
        "td,dq->tq", mixed_grad_b, wo_t, preferred_element_type=jnp.float32
    ).astype(jnp.bfloat16)
    query_grad, kv_terms = attend_back(
        query_b, kv_all, query_time, key_time, logsum, attn_b, attn_grad_b
    )
    kv_grad = exchange_sum(
        kv_terms.reshape(ctx_count, tok_count, 2 * kv_dim).astype(jnp.bfloat16)
    )
    query_pre = rotate_back(query_grad, cos_table, sin_table, H).astype(jnp.bfloat16)
    key_pre = rotate_back(kv_grad[:, :kv_dim], cos_table, sin_table, KVH)
    kv_pre = jnp.concatenate([key_pre, kv_grad[:, kv_dim:]], 1).astype(jnp.bfloat16)
    wq_grad_t = jnp.einsum("tq,td->qd", query_pre, normed_one_b, preferred_element_type=jnp.float32)
    wkv_grad_t = jnp.einsum("tk,td->kd", kv_pre, normed_one_b, preferred_element_type=jnp.float32)
    normed_one_grad = jnp.einsum(
        "tq,qd->td", query_pre, wq_t, preferred_element_type=jnp.float32
    ) + jnp.einsum("tk,kd->td", kv_pre, wkv_t, preferred_element_type=jnp.float32)
    rows_back, gain_term_one = norm_backward(rows_in, scale_one, gain_one, normed_one_grad)
    input_grad = mixed_grad + rows_back
    small_grads = jnp.concatenate(
        [
            g.astype(jnp.bfloat16).reshape(ctx_count, -1, fsdp_count * row_d)
            for g in (wq_grad_t, wkv_grad_t, wo_grad_t)
        ],
        1,
    )
    small_grads = small_grads.reshape(ctx_count, col_s, fsdp_count, row_d).transpose(2, 0, 1, 3)
    gain_grads = jnp.stack([gain_term_one, gain_term_two]).reshape(2, ctx_count, -1)
    gain_grads = gain_grads.transpose(1, 0, 2).reshape(ctx_count, -1).astype(jnp.bfloat16)
    gain_pad = (n_rows - cut_small) * lanes - gain_flat.size
    gain_grads = jnp.pad(gain_grads, ((0, 0), (0, gain_pad))).reshape(1, ctx_count, -1, lanes)
    down_pieces = wdown_grad_t.astype(jnp.bfloat16).reshape(ctx_count, col_d, fsdp_count, lanes)
    pieces = jnp.concatenate(
        [
            fold(wgu_grad.astype(jnp.bfloat16), fsdp_count, ctx_count).reshape(
                fsdp_count, ctx_count, n_gu, lanes
            ),
            down_pieces.transpose(2, 0, 1, 3),
            small_grads.reshape(fsdp_count, ctx_count, n_small, lanes),
            jnp.broadcast_to(gain_grads, (fsdp_count,) + gain_grads.shape[1:]),
        ],
        2,
    )
    owned = scatter_sum(pieces) * grad_scale
    small_owned = owned[cut_down:cut_small].reshape(-1, row_d).T
    owned_grads = (
        small_owned[:, :col_q],
        small_owned[:, col_q : col_q + col_k],
        small_owned[:, col_q + col_k :],
        owned[:n_gu].reshape(row_d, col_g),
        owned[n_gu:cut_down].T,
    )
    gains_owned = owned[cut_small:].reshape(-1)[: gain_flat.size].reshape(2, -1)
    return (
        result[None],
        input_grad[None],
        owned_grads[0],
        owned_grads[1],
        owned_grads[2],
        owned_grads[3],
        owned_grads[4],
        gains_owned,
    )


def solution(mesh):
    return jax.shard_map(
        body,
        mesh=mesh,
        in_specs=(
            P("fsdp", "ctx", None),
            P("fsdp", "ctx"),
            P("fsdp", None),
            P(None, "ctx"),
            P("fsdp", "ctx"),
            P("fsdp", "ctx"),
            P("fsdp", "ctx"),
            P("fsdp", "ctx"),
            P("fsdp", "ctx"),
            P("fsdp", "ctx", None),
        ),
        out_specs=(
            P("fsdp", "ctx", None),
            P("fsdp", "ctx", None),
            P("fsdp", "ctx"),
            P("fsdp", "ctx"),
            P("fsdp", "ctx"),
            P("fsdp", "ctx"),
            P("fsdp", "ctx"),
            P(None, "ctx"),
        ),
        check_vma=False,
    )
```

```python
import functools
import math

import jax
import jax.numpy as jnp
from jax import lax
from jax.experimental import pallas as pl
from jax.experimental.pallas import tpu as pltpu
from jax.sharding import PartitionSpec as P

H = 9
KVH = 3
HD = 64
FF = 1536


EPSILON = 1e-05
THETA = 100000.0

MESH_ID = pl.DeviceIdType.MESH
PAIR = 2


def greet(peers):
    barrier = pltpu.get_barrier_semaphore()
    for peer in peers:
        pl.semaphore_signal(barrier, inc=1, device_id=peer, device_id_type=MESH_ID)
    pl.semaphore_wait(barrier, len(peers))


class Place:
    def __init__(self, fsdp, ctx):
        self.nk, self.nx = PAIR, fsdp // PAIR
        self.ny, self.nz = PAIR, ctx // PAIR
        f = lax.axis_index("fsdp")
        c = lax.axis_index("ctx")
        self.f, self.c = f, c
        self.x, self.k = f // self.nk, f % self.nk
        self.z, self.y = c // self.ny, c % self.ny

    def rel(self, dx=0, dk=0, dz=0, dy=0):
        fx = (self.x + dx) % self.nx if dx else self.x
        fk = (self.k + dk) % self.nk if dk else self.k
        cz = (self.z + dz) % self.nz if dz else self.z
        cy = (self.y + dy) % self.ny if dy else self.y
        return (fx * self.nk + fk, cz * self.ny + cy)

    def peers(self):
        return (
            [self.rel(dx=d) for d in range(1, self.nx)]
            + [self.rel(dk=d) for d in range(1, self.nk)]
            + [self.rel(dz=d) for d in range(1, self.nz)]
            + [self.rel(dy=d) for d in range(1, self.ny)]
        )


def gather_kernel(fsdp, ctx, w_ref, h_ref, wout, hout, wsend, wrecv, hsend, hrecv, own_sem):
    me = Place(fsdp, ctx)
    nx, nk, nz, ny = me.nx, me.nk, me.nz, me.ny
    own_w = pltpu.make_async_copy(w_ref, wout.at[me.f, me.c], own_sem.at[0])
    own_h = pltpu.make_async_copy(h_ref, hout.at[me.c], own_sem.at[1])
    own_w.start()
    own_h.start()
    greet(me.peers())
    sends = []

    def push_w(kx, kk, kz, ky, stage, step, src=None):
        f, c = me.rel(dx=kx, dk=kk, dz=kz, dy=ky)
        offs = {stage: step}
        dest = me.rel(**offs)
        new = dict(dx=kx, dk=kk, dz=kz, dy=ky)
        size = dict(dx=nx, dk=nk, dz=nz, dy=ny)[stage]
        new[stage] = (new[stage] - step) % size
        slot = ((new["dx"] * nk + new["dk"]) * nz + new["dz"]) * ny + new["dy"]
        copy = pltpu.make_async_remote_copy(
            src_ref=wout.at[f, c] if src is None else src,
            dst_ref=wout.at[f, c],
            send_sem=wsend.at[slot],
            recv_sem=wrecv.at[slot],
            device_id=dest,
            device_id_type=MESH_ID,
        )
        copy.start()
        sends.append(copy)

    def wait_w(kx, kk, kz, ky):
        f, c = me.rel(dx=kx, dk=kk, dz=kz, dy=ky)
        slot = ((kx * nk + kk) * nz + kz) * ny + ky
        pltpu.make_async_remote_copy(
            src_ref=wout.at[f, c],
            dst_ref=wout.at[f, c],
            send_sem=wsend.at[slot],
            recv_sem=wrecv.at[slot],
            device_id=me.rel(dk=1),
            device_id_type=MESH_ID,
        ).wait_recv()

    def push_h(kz, ky, stage, step, src=None):
        c = me.rel(dz=kz, dy=ky)[1]
        dest = me.rel(**{stage: step})
        new = dict(dz=kz, dy=ky)
        new[stage] = (new[stage] - step) % dict(dz=nz, dy=ny)[stage]
        slot = new["dz"] * ny + new["dy"]
        copy = pltpu.make_async_remote_copy(
            src_ref=hout.at[c] if src is None else src,
            dst_ref=hout.at[c],
            send_sem=hsend.at[slot],
            recv_sem=hrecv.at[slot],
            device_id=dest,
            device_id_type=MESH_ID,
        )
        copy.start()
        sends.append(copy)

    def wait_h(kz, ky):
        c = me.rel(dz=kz, dy=ky)[1]
        slot = kz * ny + ky
        pltpu.make_async_remote_copy(
            src_ref=hout.at[c],
            dst_ref=hout.at[c],
            send_sem=hsend.at[slot],
            recv_sem=hrecv.at[slot],
            device_id=me.rel(dk=1),
            device_id_type=MESH_ID,
        ).wait_recv()

    if nz > 1:
        push_w(0, 0, 0, 0, "dz", 1, w_ref)
    for d in range(1, nx):
        push_w(0, 0, 0, 0, "dx", d, w_ref)
    for d in range(1, ny):
        push_w(0, 0, 0, 0, "dy", d, w_ref)
    for d in range(1, nk):
        push_w(0, 0, 0, 0, "dk", d, w_ref)
    if nz > 1:
        push_h(0, 0, "dz", 1, h_ref)
    for d in range(1, ny):
        push_h(0, 0, "dy", d, h_ref)
    for kz in range(nz - 1, 0, -1):
        wait_w(0, 0, kz, 0)
        if kz > 1:
            push_w(0, 0, kz, 0, "dz", 1)
        for d in range(1, nx):
            push_w(0, 0, kz, 0, "dx", d)
        for d in range(1, ny):
            push_w(0, 0, kz, 0, "dy", d)
        for d in range(1, nk):
            push_w(0, 0, kz, 0, "dk", d)
        for ky in range(1, ny):
            before = (kz + 1) % nz
            wait_w(0, 0, before, ky)
            for d in range(1, nx):
                push_w(0, 0, before, ky, "dx", d)
            for d in range(1, nk):
                push_w(0, 0, before, ky, "dk", d)
        wait_h(kz, 0)
        if kz > 1:
            push_h(kz, 0, "dz", 1)
        for d in range(1, ny):
            push_h(kz, 0, "dy", d)
    for ky in range(1, ny):
        last = 1 % nz
        wait_w(0, 0, last, ky)
        for d in range(1, nx):
            push_w(0, 0, last, ky, "dx", d)
        for d in range(1, nk):
            push_w(0, 0, last, ky, "dk", d)
        for kz in range(nz):
            wait_h(kz, ky)
    arrival = [(0, 0)]
    for kz in range(nz - 1, 0, -1):
        arrival += [(kz, 0)] + [((kz + 1) % nz, ky) for ky in range(1, ny)]
    arrival += [(1 % nz, ky) for ky in range(1, ny)]
    for kx in range(1, nx):
        for kz, ky in arrival:
            wait_w(kx, 0, kz, ky)
            for d in range(1, nk):
                push_w(kx, 0, kz, ky, "dk", d)
    for kk in range(1, nk):
        for kx in range(nx):
            for ky in range(ny):
                for kz in range(nz):
                    wait_w(kx, kk, kz, ky)
    for copy in sends:
        copy.wait_send()
    own_w.wait()
    own_h.wait()


def gather_all(packed, rows):
    fsdp, ctx = lax.axis_size("fsdp"), lax.axis_size("ctx")
    return pl.pallas_call(
        functools.partial(gather_kernel, fsdp, ctx),
        out_shape=(
            jax.ShapeDtypeStruct((fsdp, ctx) + packed.shape, packed.dtype),
            jax.ShapeDtypeStruct((ctx,) + rows.shape, rows.dtype),
        ),
        in_specs=[pl.BlockSpec(memory_space=pltpu.VMEM)] * 2,
        out_specs=[pl.BlockSpec(memory_space=pl.ANY)] * 2,
        scratch_shapes=[
            pltpu.SemaphoreType.DMA((fsdp * ctx,)),
            pltpu.SemaphoreType.DMA((fsdp * ctx,)),
            pltpu.SemaphoreType.DMA((ctx,)),
            pltpu.SemaphoreType.DMA((ctx,)),
            pltpu.SemaphoreType.DMA((2,)),
        ],
        compiler_params=pltpu.CompilerParams(collective_id=0, has_side_effects=True),
    )(packed, rows)


def exchange_kernel(fsdp, ctx, part_ref, out_ref, held_y, held_z, send, recv_y, recv_z):
    me = Place(fsdp, ctx)
    nz, ny = me.nz, me.ny
    greet(
        [me.rel(dz=d) for d in range(1, nz)] + [me.rel(dy=d) for d in range(1, ny)],
    )
    sends = []
    y_copies, z_copies = {}, {}
    order_z = list(range(1, nz)) + [0]
    for dz in order_z:
        for dy in range(1, ny):
            slot = (dy - 1) * nz + dz
            copy = pltpu.make_async_remote_copy(
                src_ref=part_ref.at[me.rel(dz=dz, dy=dy)[1]],
                dst_ref=held_y.at[slot],
                send_sem=send.at[len(sends)],
                recv_sem=recv_y.at[slot],
                device_id=me.rel(dy=dy),
                device_id_type=MESH_ID,
            )
            copy.start()
            sends.append(copy)
            y_copies[dz, dy] = copy

    def y_sum(dz):
        total = part_ref[me.rel(dz=dz)[1]].astype(jnp.float32)
        for dy in range(1, ny):
            y_copies[dz, dy].wait_recv()
            total = total + held_y[(dy - 1) * nz + dz].astype(jnp.float32)
        return total

    for dz in range(1, nz):
        held_y[dz] = y_sum(dz).astype(held_y.dtype)
        copy = pltpu.make_async_remote_copy(
            src_ref=held_y.at[dz],
            dst_ref=held_z.at[dz - 1],
            send_sem=send.at[len(sends)],
            recv_sem=recv_z.at[dz - 1],
            device_id=me.rel(dz=dz),
            device_id_type=MESH_ID,
        )
        copy.start()
        sends.append(copy)
        z_copies[dz] = copy
    total = y_sum(0)
    for dz in range(1, nz):
        z_copies[dz].wait_recv()
        total = total + held_z[dz - 1].astype(jnp.float32)
    out_ref[...] = total
    for copy in sends:
        copy.wait_send()


def exchange_sum(parts):
    fsdp, ctx = lax.axis_size("fsdp"), lax.axis_size("ctx")
    counts = ((PAIR - 1) * (ctx // PAIR), ctx // PAIR - 1)
    return pl.pallas_call(
        functools.partial(exchange_kernel, fsdp, ctx),
        out_shape=jax.ShapeDtypeStruct(parts.shape[1:], jnp.float32),
        in_specs=[pl.BlockSpec(memory_space=pltpu.VMEM)],
        out_specs=pl.BlockSpec(memory_space=pltpu.VMEM),
        scratch_shapes=[pltpu.VMEM((n,) + parts.shape[1:], parts.dtype) for n in counts]
        + [pltpu.SemaphoreType.DMA((n,)) for n in (sum(counts),) + counts],
        compiler_params=pltpu.CompilerParams(
            collective_id=1, has_side_effects=True, vmem_limit_bytes=48 * 2**20
        ),
    )(parts)


def scatter_kernel(
    fsdp, ctx, g_ref, out_ref, held_k, held_x, held_y, held_z, send, recv_k, recv_x, recv_y, recv_z
):
    me = Place(fsdp, ctx)
    nx, nz, ny = me.nx, me.nz, me.ny
    greet(me.peers())
    sends = []

    def push(src, dst, dst_sem, dest):
        copy = pltpu.make_async_remote_copy(
            src_ref=src,
            dst_ref=dst,
            send_sem=send.at[len(sends)],
            recv_sem=dst_sem,
            device_id=dest,
            device_id_type=MESH_ID,
        )
        copy.start()
        sends.append(copy)

    def wait(ref, sem):
        pltpu.make_async_remote_copy(
            src_ref=ref,
            dst_ref=ref,
            send_sem=sem,
            recv_sem=sem,
            device_id=me.rel(dk=1),
            device_id_type=MESH_ID,
        ).wait_recv()

    order_x = list(range(1, nx)) + [0]
    order_c = [(dy, dz) for dy in list(range(1, ny)) + [0] for dz in list(range(1, nz)) + [0]]
    for dx in order_x:
        for dy, dz in order_c:
            f, c = me.rel(dx=dx, dk=1, dz=dz, dy=dy)
            slot = (dx * nz + dz) * ny + dy
            push(g_ref.at[f, c], held_k.at[slot], recv_k.at[slot], me.rel(dk=1))

    def local_sum(dx, dz, dy):
        f, c = me.rel(dx=dx, dz=dz, dy=dy)
        slot = (dx * nz + dz) * ny + dy
        wait(held_k.at[slot], recv_k.at[slot])
        return g_ref[f, c].astype(jnp.float32) + held_k[slot].astype(jnp.float32), slot

    for dx in order_x[:-1]:
        for dy, dz in order_c:
            total, slot = local_sum(dx, dz, dy)
            held_k[slot] = total.astype(held_k.dtype)
            there = ((dx - 1) * nz + dz) * ny + dy
            push(held_k.at[slot], held_x.at[there], recv_x.at[there], me.rel(dx=dx))

    def x_sum(dz, dy):
        total, slot = local_sum(0, dz, dy)
        for dx in range(1, nx):
            there = ((dx - 1) * nz + dz) * ny + dy
            wait(held_x.at[there], recv_x.at[there])
            total = total + held_x[there].astype(jnp.float32)
        return total, slot

    for dy in range(1, ny):
        for dz in list(range(1, nz)) + [0]:
            total, slot = x_sum(dz, dy)
            held_k[slot] = total.astype(held_k.dtype)
            there = (dy - 1) * nz + dz
            push(held_k.at[slot], held_y.at[there], recv_y.at[there], me.rel(dy=dy))

    def y_sum(dz):
        total, slot = x_sum(dz, 0)
        for dy in range(1, ny):
            there = (dy - 1) * nz + dz
            wait(held_y.at[there], recv_y.at[there])
            total = total + held_y[there].astype(jnp.float32)
        return total, slot

    for dz in range(1, nz):
        total, slot = y_sum(dz)
        held_k[slot] = total.astype(held_k.dtype)
        push(held_k.at[slot], held_z.at[dz - 1], recv_z.at[dz - 1], me.rel(dz=dz))
    total, slot = y_sum(0)
    for dz in range(1, nz):
        wait(held_z.at[dz - 1], recv_z.at[dz - 1])
        total = total + held_z[dz - 1].astype(jnp.float32)
    out_ref[...] = total
    for copy in sends:
        copy.wait_send()


def scatter_sum(grads):
    fsdp, ctx, rows, lanes = grads.shape
    nx, nz, ny = fsdp // PAIR, ctx // PAIR, PAIR
    counts = (nx * ctx, (nx - 1) * ctx, (ny - 1) * nz, nz - 1)
    return pl.pallas_call(
        functools.partial(scatter_kernel, fsdp, ctx),
        out_shape=jax.ShapeDtypeStruct((rows, lanes), jnp.float32),
        in_specs=[pl.BlockSpec(memory_space=pltpu.VMEM)],
        out_specs=pl.BlockSpec(memory_space=pltpu.VMEM),
        scratch_shapes=[pltpu.VMEM((n, rows, lanes), grads.dtype) for n in counts]
        + [pltpu.SemaphoreType.DMA((n,)) for n in (sum(counts),) + counts],
        compiler_params=pltpu.CompilerParams(
            collective_id=2, has_side_effects=True, vmem_limit_bytes=48 * 2**20
        ),
    )(grads)


def unfold(pieces, row_count, col_count):
    fsdp, ctx = pieces.shape[:2]
    shaped = pieces.reshape(fsdp, ctx, row_count, col_count)
    return shaped.transpose(0, 2, 1, 3).reshape(fsdp * row_count, ctx * col_count)


def fold(whole, fsdp, ctx):
    row_count, col_count = whole.shape
    shaped = whole.reshape(fsdp, row_count // fsdp, ctx, col_count // ctx)
    return shaped.transpose(0, 2, 1, 3)


def block_times(pair_row, block_len, ctx_count):
    within_ids = jnp.arange(2 * block_len, dtype=jnp.int32)[None, :]
    first_block = pair_row[:, None]
    block_ids = jnp.where(within_ids < block_len, first_block, 2 * ctx_count - 1 - first_block)
    return (block_ids * block_len + within_ids % block_len).reshape(-1)


def rope_tables(token_pos, head_size):
    half_size = head_size // 2
    freq_vec = THETA ** (-(jnp.arange(half_size, dtype=jnp.float32) * 2.0) / head_size)
    angles = token_pos.astype(jnp.float32)[:, None] * freq_vec[None, :]
    cos_half = jnp.cos(angles)
    sin_half = jnp.sin(angles)
    return (jnp.concatenate([cos_half, cos_half], 1), jnp.concatenate([sin_half, sin_half], 1))


def rotate(values, cos_table, sin_table, head_count):
    row_count = values.shape[0]
    shaped = values.reshape(row_count, head_count, -1)
    half_size = shaped.shape[2] // 2
    turned = jnp.concatenate([-shaped[:, :, half_size:], shaped[:, :, :half_size]], 2)
    return (shaped * cos_table[:, None, :] + turned * sin_table[:, None, :]).reshape(row_count, -1)


def rotate_back(grad_vals, cos_table, sin_table, head_count):
    row_count = grad_vals.shape[0]
    shaped = grad_vals.reshape(row_count, head_count, -1)
    half_size = shaped.shape[2] // 2
    scaled = shaped * sin_table[:, None, :]
    turned = jnp.concatenate([scaled[:, :, half_size:], -scaled[:, :, :half_size]], 2)
    return (shaped * cos_table[:, None, :] + turned).reshape(row_count, -1)


def norm_forward(values, gain_vec):
    inv_scale = lax.rsqrt(jnp.mean(values * values, axis=1, keepdims=True) + EPSILON)
    return (values * inv_scale * gain_vec[None, :], inv_scale)


def norm_backward(values, inv_scale, gain_vec, grad_out):
    weighted = grad_out * gain_vec[None, :]
    gain_grad = jnp.sum(grad_out * values * inv_scale, axis=0)
    inner_mean = jnp.mean(weighted * values, axis=1, keepdims=True)
    return (inv_scale * weighted - values * inv_scale**3 * inner_mean, gain_grad)


def score_block(query_grp, key_blk, query_time, key_time):
    scores = jnp.einsum(
        "qkgd,skd->kgqs", query_grp, key_blk, preferred_element_type=jnp.float32
    ) * HD ** (-0.5)
    key_mask = key_time[None, None, None, :] <= query_time[None, None, :, None]
    return (scores, key_mask)


def attend(query_b, kv_all, query_time, key_time):
    tok_count = query_b.shape[0]
    length = kv_all.shape[0]
    width = math.gcd(length, 1024)
    block_count = length // width
    group_size = H // KVH
    query_grp = query_b.reshape(tok_count, KVH, group_size, HD)
    kv_blocks = kv_all.reshape(block_count, width, 2, KVH, HD)
    time_blocks = key_time.reshape(block_count, width)

    def total_step(running, block_in):
        kv_blk, time_blk = block_in
        scores, key_mask = score_block(query_grp, kv_blk[:, 0], query_time, time_blk)
        return (running + jnp.sum(jnp.where(key_mask, jnp.exp(scores), 0.0), axis=3), None)

    totals = lax.scan(
        total_step, jnp.zeros((KVH, group_size, tok_count), jnp.float32), (kv_blocks, time_blocks)
    )[0]
    logsum = jnp.log(totals)

    def output_step(running, block_in):
        kv_blk, time_blk = block_in
        scores, key_mask = score_block(query_grp, kv_blk[:, 0], query_time, time_blk)
        prob_b = jnp.where(key_mask, jnp.exp(scores - logsum[:, :, :, None]), 0.0).astype(
            jnp.bfloat16
        )
        part_out = jnp.einsum(
            "kgqs,skd->qkgd", prob_b, kv_blk[:, 1], preferred_element_type=jnp.float32
        )
        return (running + part_out, None)

    attn_out = lax.scan(
        output_step,
        jnp.zeros((tok_count, KVH, group_size, HD), jnp.float32),
        (kv_blocks, time_blocks),
    )[0]
    return (attn_out.reshape(tok_count, -1).astype(jnp.bfloat16), logsum)


def attend_back(query_b, kv_all, query_time, key_time, logsum, attn_b, attn_grad_b):
    tok_count = query_b.shape[0]
    length = kv_all.shape[0]
    width = math.gcd(length, 1024)
    block_count = length // width
    group_size = H // KVH
    query_grp = query_b.reshape(tok_count, KVH, group_size, HD)
    grad_grp = attn_grad_b.reshape(tok_count, KVH, group_size, HD)
    product = attn_grad_b.astype(jnp.float32) * attn_b.astype(jnp.float32)
    delta_sum = jnp.sum(product.reshape(tok_count, KVH, group_size, HD), axis=3).transpose(1, 2, 0)
    kv_blocks = kv_all.reshape(block_count, width, 2, KVH, HD)
    time_blocks = key_time.reshape(block_count, width)

    def back_step(running, block_in):
        kv_blk, time_blk = block_in
        scores, key_mask = score_block(query_grp, kv_blk[:, 0], query_time, time_blk)
        prob_f = jnp.where(key_mask, jnp.exp(scores - logsum[:, :, :, None]), 0.0)
        prob_grad = jnp.einsum(
            "qkgd,skd->kgqs", grad_grp, kv_blk[:, 1], preferred_element_type=jnp.float32
        )
        score_grad = (prob_f * (prob_grad - delta_sum[:, :, :, None]) * HD ** (-0.5)).astype(
            jnp.bfloat16
        )
        query_next = running + jnp.einsum(
            "kgqs,skd->qkgd", score_grad, kv_blk[:, 0], preferred_element_type=jnp.float32
        )
        key_grad = jnp.einsum(
            "kgqs,qkgd->skd", score_grad, query_grp, preferred_element_type=jnp.float32
        )
        value_grad = jnp.einsum(
            "kgqs,qkgd->skd",
            prob_f.astype(jnp.bfloat16),
            grad_grp,
            preferred_element_type=jnp.float32,
        )
        return (
            query_next,
            jnp.concatenate([key_grad.reshape(width, -1), value_grad.reshape(width, -1)], 1),
        )

    query_grad, kv_grad = lax.scan(
        back_step,
        jnp.zeros((tok_count, KVH, group_size, HD), jnp.float32),
        (kv_blocks, time_blocks),
    )
    return (query_grad.reshape(tok_count, -1), kv_grad.reshape(length, -1))


def body(
    hidden_in,
    positions,
    block_pairs,
    norm_gains,
    w_query,
    w_kv,
    w_out,
    w_gate_up,
    w_down,
    output_grad,
):
    tok_count = hidden_in.shape[1]
    ctx_count = lax.axis_size("ctx")
    block_len = tok_count // 2
    kv_dim = KVH * HD
    grad_scale = 1.0 / math.sqrt(lax.axis_size("fsdp") * ctx_count * tok_count)
    fsdp_count = lax.axis_size("fsdp")
    width = hidden_in.shape[2]
    row_d, col_q = w_query.shape
    col_k, col_o, col_g = w_kv.shape[1], w_out.shape[1], w_gate_up.shape[1]
    lanes, col_d = w_down.shape
    small = jnp.concatenate([w_query.T, w_kv.T, w_out.T], 0)
    gain_flat = norm_gains.reshape(-1)
    n_gu = row_d * col_g // lanes
    n_small = small.size // lanes
    n_gain = -(-gain_flat.size // lanes)
    cut_down, cut_small = n_gu + col_d, n_gu + col_d + n_small
    n_rows = -(-(cut_small + n_gain) // 16) * 16
    gain_rows = jnp.pad(gain_flat, (0, (n_rows - cut_small) * lanes - gain_flat.size))
    packed = jnp.concatenate(
        [
            w_gate_up.reshape(n_gu, lanes),
            w_down.T,
            small.reshape(n_small, lanes),
            gain_rows.reshape(-1, lanes),
        ],
        0,
    )
    pos_cols = jnp.stack([positions[0] // 128, positions[0] % 128], 1).astype(jnp.bfloat16)
    spare = (-(width + 2)) % 128
    rows_b = jnp.concatenate([hidden_in[0], jnp.pad(pos_cols, ((0, 0), (0, spare)))], 1)
    gathered, rows_all = gather_all(packed, rows_b)
    wgu_full = unfold(gathered[:, :, :n_gu], row_d, col_g)
    wdown_t = gathered[:, :, n_gu:cut_down].transpose(1, 2, 0, 3).reshape(ctx_count * col_d, -1)
    col_s = small.shape[0]
    small_all = gathered[:, :, cut_down:cut_small].reshape(fsdp_count, ctx_count, col_s, row_d)
    small_all = small_all.transpose(1, 2, 0, 3).reshape(ctx_count, col_s, fsdp_count * row_d)
    wq_t = small_all[:, :col_q].reshape(ctx_count * col_q, -1)
    wkv_t = small_all[:, col_q : col_q + col_k].reshape(ctx_count * col_k, -1)
    wo_t = small_all[:, col_q + col_k :].reshape(ctx_count * col_o, -1)
    gain_all = gathered[0, :, cut_small:].reshape(ctx_count, -1)[:, : gain_flat.size]
    gain_all = gain_all.reshape(ctx_count, 2, -1).transpose(1, 0, 2).reshape(2, -1)
    gain_one = gain_all[0].astype(jnp.float32)
    gain_two = gain_all[1].astype(jnp.float32)
    rows_in = hidden_in[0].astype(jnp.float32)
    normed_one, scale_one = norm_forward(rows_in, gain_one)
    normed_one_b = normed_one.astype(jnp.bfloat16)
    query = jnp.einsum("td,qd->tq", normed_one_b, wq_t, preferred_element_type=jnp.float32)
    cos_table, sin_table = rope_tables(positions[0], HD)
    query_b = rotate(query, cos_table, sin_table, H).astype(jnp.bfloat16)
    rows_all = rows_all.reshape(ctx_count * tok_count, -1)
    normed_all = norm_forward(rows_all[:, :width].astype(jnp.float32), gain_one)[0]
    kv_proj = jnp.einsum(
        "td,kd->tk", normed_all.astype(jnp.bfloat16), wkv_t, preferred_element_type=jnp.float32
    )
    pos_all = rows_all[:, width : width + 2].astype(jnp.float32)
    cos_all, sin_all = rope_tables(pos_all[:, 0] * 128.0 + pos_all[:, 1], HD)
    key_b = rotate(kv_proj[:, :kv_dim], cos_all, sin_all, KVH).astype(jnp.bfloat16)
    kv_all = jnp.concatenate([key_b, kv_proj[:, kv_dim:].astype(jnp.bfloat16)], 1)
    key_time = block_times(block_pairs[0], block_len, ctx_count)
    query_time = lax.dynamic_slice_in_dim(key_time, lax.axis_index("ctx") * tok_count, tok_count)
    attn_b, logsum = attend(query_b, kv_all, query_time, key_time)
    mixed = rows_in + jnp.einsum("tq,dq->td", attn_b, wo_t, preferred_element_type=jnp.float32)
    normed_two, scale_two = norm_forward(mixed, gain_two)
    normed_two_b = normed_two.astype(jnp.bfloat16)
    gate_up = jnp.dot(normed_two_b, wgu_full, preferred_element_type=jnp.float32)
    gate_part = gate_up[:, :FF]
    up_part = gate_up[:, FF:]
    sig_gate = jax.nn.sigmoid(gate_part)
    silu_gate = gate_part * sig_gate
    act_b = (silu_gate * up_part).astype(jnp.bfloat16)
    down_out = jnp.einsum("tf,df->td", act_b, wdown_t, preferred_element_type=jnp.float32)
    result = (mixed + down_out).astype(jnp.bfloat16)
    grad_b = output_grad[0]
    act_grad = jnp.einsum("td,df->tf", grad_b, wdown_t, preferred_element_type=jnp.float32)
    wdown_grad_t = jnp.einsum("td,tf->df", grad_b, act_b, preferred_element_type=jnp.float32)
    gate_grad = act_grad * up_part * sig_gate * (1.0 + gate_part * (1.0 - sig_gate))
    gu_grad_b = jnp.concatenate([gate_grad, act_grad * silu_gate], 1).astype(jnp.bfloat16)
    wgu_grad = jnp.einsum("td,tf->df", normed_two_b, gu_grad_b, preferred_element_type=jnp.float32)
    normed_two_grad = jnp.einsum(
        "tf,df->td", gu_grad_b, wgu_full, preferred_element_type=jnp.float32
    )
    mixed_back, gain_term_two = norm_backward(mixed, scale_two, gain_two, normed_two_grad)
    mixed_grad = grad_b.astype(jnp.float32) + mixed_back
    mixed_grad_b = mixed_grad.astype(jnp.bfloat16)
    wo_grad_t = jnp.einsum("td,tq->dq", mixed_grad_b, attn_b, preferred_element_type=jnp.float32)
    attn_grad_b = jnp.einsum(
        "td,dq->tq", mixed_grad_b, wo_t, preferred_element_type=jnp.float32
    ).astype(jnp.bfloat16)
    query_grad, kv_terms = attend_back(
        query_b, kv_all, query_time, key_time, logsum, attn_b, attn_grad_b
    )
    kv_grad = exchange_sum(
        kv_terms.reshape(ctx_count, tok_count, 2 * kv_dim).astype(jnp.bfloat16)
    )
    query_pre = rotate_back(query_grad, cos_table, sin_table, H).astype(jnp.bfloat16)
    key_pre = rotate_back(kv_grad[:, :kv_dim], cos_table, sin_table, KVH)
    kv_pre = jnp.concatenate([key_pre, kv_grad[:, kv_dim:]], 1).astype(jnp.bfloat16)
    wq_grad_t = jnp.einsum("tq,td->qd", query_pre, normed_one_b, preferred_element_type=jnp.float32)
    wkv_grad_t = jnp.einsum("tk,td->kd", kv_pre, normed_one_b, preferred_element_type=jnp.float32)
    normed_one_grad = jnp.einsum(
        "tq,qd->td", query_pre, wq_t, preferred_element_type=jnp.float32
    ) + jnp.einsum("tk,kd->td", kv_pre, wkv_t, preferred_element_type=jnp.float32)
    rows_back, gain_term_one = norm_backward(rows_in, scale_one, gain_one, normed_one_grad)
    input_grad = mixed_grad + rows_back
    small_grads = jnp.concatenate(
        [
            g.astype(jnp.bfloat16).reshape(ctx_count, -1, fsdp_count * row_d)
            for g in (wq_grad_t, wkv_grad_t, wo_grad_t)
        ],
        1,
    )
    small_grads = small_grads.reshape(ctx_count, col_s, fsdp_count, row_d).transpose(2, 0, 1, 3)
    gain_grads = jnp.stack([gain_term_one, gain_term_two]).reshape(2, ctx_count, -1)
    gain_grads = gain_grads.transpose(1, 0, 2).reshape(ctx_count, -1).astype(jnp.bfloat16)
    gain_pad = (n_rows - cut_small) * lanes - gain_flat.size
    gain_grads = jnp.pad(gain_grads, ((0, 0), (0, gain_pad))).reshape(1, ctx_count, -1, lanes)
    down_pieces = wdown_grad_t.astype(jnp.bfloat16).reshape(ctx_count, col_d, fsdp_count, lanes)
    pieces = jnp.concatenate(
        [
            fold(wgu_grad.astype(jnp.bfloat16), fsdp_count, ctx_count).reshape(
                fsdp_count, ctx_count, n_gu, lanes
            ),
            down_pieces.transpose(2, 0, 1, 3),
            small_grads.reshape(fsdp_count, ctx_count, n_small, lanes),
            jnp.broadcast_to(gain_grads, (fsdp_count,) + gain_grads.shape[1:]),
        ],
        2,
    )
    owned = scatter_sum(pieces) * grad_scale
    small_owned = owned[cut_down:cut_small].reshape(-1, row_d).T
    owned_grads = (
        small_owned[:, :col_q],
        small_owned[:, col_q : col_q + col_k],
        small_owned[:, col_q + col_k :],
        owned[:n_gu].reshape(row_d, col_g),
        owned[n_gu:cut_down].T,
    )
    gains_owned = owned[cut_small:].reshape(-1)[: gain_flat.size].reshape(2, -1)
    return (
        result[None],
        input_grad[None],
        owned_grads[0],
        owned_grads[1],
        owned_grads[2],
        owned_grads[3],
        owned_grads[4],
        gains_owned,
    )


def solution(mesh):
    return jax.shard_map(
        body,
        mesh=mesh,
        in_specs=(
            P("fsdp", "ctx", None),
            P("fsdp", "ctx"),
            P("fsdp", None),
            P(None, "ctx"),
            P("fsdp", "ctx"),
            P("fsdp", "ctx"),
            P("fsdp", "ctx"),
            P("fsdp", "ctx"),
            P("fsdp", "ctx"),
            P("fsdp", "ctx", None),
        ),
        out_specs=(
            P("fsdp", "ctx", None),
            P("fsdp", "ctx", None),
            P("fsdp", "ctx"),
            P("fsdp", "ctx"),
            P("fsdp", "ctx"),
            P("fsdp", "ctx"),
            P("fsdp", "ctx"),
            P(None, "ctx"),
        ),
        check_vma=False,
    )
```
